256 devices in a mesh: seq: 64 (over z, x, core), dp: 4 (over y).
Axes of the slice: x: 4, y: 4, z: 8, core: 2. Of those that a mesh axis runs over, the one named last changes fastest.
Arguments:
- queries: bfloat16 [4, 8192, 2048], P('dp', 'seq'), may hold values from -6 to 6
- keys: bfloat16 [4, 8192, 2048], P('dp', 'seq'), may hold values from -6 to 6
- values: bfloat16 [4, 8192, 2048], P('dp', 'seq'), may hold values from -6 to 6
- out_grad: bfloat16 [4, 8192, 2048], P('dp', 'seq'), may hold values from -6 to 6
- gain: float32 [2048], replicated, may hold values from 0.1 to 1.9
Outputs:
- normed_out: bfloat16 [4, 8192, 2048], P('dp', 'seq')
- query_grad: bfloat16 [4, 8192, 2048], P('dp', 'seq')
- key_grad: bfloat16 [4, 8192, 2048], P('dp', 'seq')
- value_grad: bfloat16 [4, 8192, 2048], P('dp', 'seq')
- gain_grad: float32 [2048], replicated
The draws below stay inside these ranges and needn't reach their ends.
All inputs are finite; a program needn't handle non-finite values.
Results may differ from the reference program's by a relative error of at most 0.0085.
Values sent between devices are 32-bit elements; how exact they have to be, the bound alone decides.
No kernel may reach another device: no remote copies, remote signals or barrier semaphores. Data moves between devices by JAX's collectives and lax.ppermute only.
A program may use at most 192 MiB of HBM per device.

```python
import functools
import math
import jax
import jax.numpy as jnp
from jax import lax

HEADS = 16
HEAD = 128
GROUP = 128
WIDTH = 2048
SEQLEN = 8192
BATCH = 4


def steps_of(rng, dims, cuts, smallest, top_value):
    loudness = 1.0
    for position, shards_of in cuts:
        steps = jax.random.uniform(jax.random.fold_in(jax.random.fold_in(rng, 6), position), (shards_of,), jnp.float32, smallest / len(cuts), top_value / len(cuts))
        loudness = loudness * jnp.repeat(jnp.exp(steps), dims[position] // shards_of).reshape((-1,) + (1,) * (len(dims) - 1 - position))
    return loudness


def gaussian(own_key, shape, deviation, reach, split=(), held_as=jnp.bfloat16):
    values = deviation * jax.random.normal(own_key, shape, jnp.float32)
    if split:
        values = values * steps_of(own_key, shape, split, -0.22, 0.18)
    return jnp.clip(values, -reach, reach).astype(held_as)


def setup_inputs(seed: int = 0) -> dict:
    splits = jax.random.split(jax.random.key(seed), 6)
    return {
        "queries": gaussian(splits[0], (BATCH, SEQLEN, WIDTH), 1.0, 6.0, ((0, 4), (1, 64))),
        "keys": gaussian(splits[1], (BATCH, SEQLEN, WIDTH), 1.0, 6.0, ((0, 4), (1, 64))),
        "values": gaussian(splits[2], (BATCH, SEQLEN, WIDTH), 1.0, 6.0, ((0, 4), (1, 64))),
        "out_grad": gaussian(splits[3], (BATCH, SEQLEN, WIDTH), 1.0, 6.0, ((0, 4), (1, 64))),
        "gain": jnp.clip(1.0 + 0.18 * jax.random.normal(splits[4], (WIDTH,), jnp.float32), 0.1, 1.9),
    }


def to_blocks(array, batch_size, block_count):
    shaped = array.reshape(batch_size, block_count, GROUP, HEADS, HEAD)
    return shaped.transpose(1, 0, 2, 3, 4)

def from_blocks(array, batch_size, seq_total):
    return array.transpose(1, 0, 2, 3, 4).reshape(batch_size, seq_total, HEADS * HEAD)

def split_state(state):
    state_high = state.astype(jnp.bfloat16)
    state_low = (state - state_high.astype(jnp.float32)).astype(jnp.bfloat16)
    return (state_high.astype(jnp.float32), state_low.astype(jnp.float32))

def forward_block(causal, gain_rows, state, inputs):
    query_rows, key_rows, value_rows, grad_rows = inputs
    query_wide = query_rows.astype(jnp.float32)
    key_wide = key_rows.astype(jnp.float32)
    value_wide = value_rows.astype(jnp.float32)
    state_high, state_low = split_state(state)
    scores = jnp.einsum('bthe,bshe->bhts', query_wide, key_wide) * causal
    weights = scores.astype(jnp.bfloat16)
    attended = jnp.einsum('bhts,bshe->bthe', weights.astype(jnp.float32), value_wide)
    attended = attended + jnp.einsum('bthe,bhef->bthf', query_wide, state_high, precision=lax.Precision.HIGHEST)
    attended = attended + jnp.einsum('bthe,bhef->bthf', query_wide, state_low, precision=lax.Precision.HIGHEST)
    mean_square = lax.optimization_barrier(jnp.mean(attended * attended, axis=-1, keepdims=True))
    inv_rms = lax.rsqrt(mean_square + 1e-05)
    normed = attended * inv_rms
    output_rows = (normed * gain_rows).astype(jnp.bfloat16)
    grad_wide = grad_rows.astype(jnp.float32)
    grad_normed = grad_wide * gain_rows
    grad_out = inv_rms * (grad_normed - normed * lax.optimization_barrier(jnp.mean(grad_normed * normed, axis=-1, keepdims=True)))
    grad_half = grad_out.astype(jnp.bfloat16)
    gain_part = lax.optimization_barrier(jnp.sum(normed * grad_wide, axis=(0, 1)))
    grad_half_wide = grad_half.astype(jnp.float32)
    mixed = (jnp.einsum('bthe,bshe->bhts', grad_half_wide, value_wide) * causal).astype(jnp.bfloat16)
    grad_query = jnp.einsum('bhts,bshe->bthe', mixed.astype(jnp.float32), key_wide)
    grad_query = grad_query + jnp.einsum('bthf,bhef->bthe', grad_half_wide, state_high, precision=lax.Precision.HIGHEST)
    grad_query = grad_query + jnp.einsum('bthf,bhef->bthe', grad_half_wide, state_low, precision=lax.Precision.HIGHEST)
    key_value = jnp.einsum('bshe,bshf->bhef', key_wide, value_wide)
    return (state + key_value, (output_rows, grad_query.astype(jnp.bfloat16), grad_half, gain_part))

def backward_block(causal, later_sum, inputs):
    query_rows, key_rows, value_rows, grad_half = inputs
    query_wide = query_rows.astype(jnp.float32)
    key_wide = key_rows.astype(jnp.float32)
    value_wide = value_rows.astype(jnp.float32)
    grad_half_wide = grad_half.astype(jnp.float32)
    later_high, later_low = split_state(later_sum)
    weights = (jnp.einsum('bthe,bshe->bhts', query_wide, key_wide) * causal).astype(jnp.bfloat16)
    mixed = (jnp.einsum('bthe,bshe->bhts', grad_half_wide, value_wide) * causal).astype(jnp.bfloat16)
    grad_key = jnp.einsum('bhts,bthe->bshe', mixed.astype(jnp.float32), query_wide)
    grad_key = grad_key + jnp.einsum('bshf,bhef->bshe', value_wide, later_high, precision=lax.Precision.HIGHEST)
    grad_key = grad_key + jnp.einsum('bshf,bhef->bshe', value_wide, later_low, precision=lax.Precision.HIGHEST)
    grad_value = jnp.einsum('bhts,bthf->bshf', weights.astype(jnp.float32), grad_half_wide)
    grad_value = grad_value + jnp.einsum('bshe,bhef->bshf', key_wide, later_high, precision=lax.Precision.HIGHEST)
    grad_value = grad_value + jnp.einsum('bshe,bhef->bshf', key_wide, later_low, precision=lax.Precision.HIGHEST)
    outer = jnp.einsum('bthe,bthf->bhef', query_wide, grad_half_wide)
    return (later_sum + outer, (grad_key.astype(jnp.bfloat16), grad_value.astype(jnp.bfloat16)))

def reference(queries, keys, values, out_grad, gain):
    batch_size = queries.shape[0]
    seq_total = queries.shape[1]
    block_count = seq_total // GROUP
    blocked = [to_blocks(a, batch_size, block_count) for a in (queries, keys, values, out_grad)]
    row_index = lax.broadcasted_iota(jnp.int32, (GROUP, GROUP), 0)
    col_index = lax.broadcasted_iota(jnp.int32, (GROUP, GROUP), 1)
    causal = (row_index >= col_index).astype(jnp.float32)
    gain_rows = gain.astype(jnp.float32).reshape(HEADS, HEAD)
    empty_state = jnp.zeros((batch_size, HEADS, HEAD, HEAD), jnp.float32)
    forward_fn = functools.partial(forward_block, causal, gain_rows)
    unused_state, results = lax.scan(forward_fn, empty_state, tuple(blocked))
    output_blocks, query_blocks, grad_blocks, gain_parts = results
    backward_fn = functools.partial(backward_block, causal)
    unused_later, grads = lax.scan(backward_fn, empty_state, (blocked[0], blocked[1], blocked[2], grad_blocks), reverse=True)
    key_blocks, value_blocks = grads
    gain_grad = (lax.optimization_barrier(jnp.sum(gain_parts, axis=0)) / math.sqrt(batch_size * seq_total)).reshape(HEADS * HEAD)
    normed_out = from_blocks(output_blocks, batch_size, seq_total)
    query_grad = from_blocks(query_blocks, batch_size, seq_total)
    key_grad = from_blocks(key_blocks, batch_size, seq_total)
    value_grad = from_blocks(value_blocks, batch_size, seq_total)
    return (normed_out, query_grad, key_grad, value_grad, gain_grad)
```

```python
import math

import jax
import jax.numpy as jnp
from jax import lax
from jax.experimental import pallas as pl
from jax.experimental.pallas import tpu as pltpu
from jax.sharding import Mesh, PartitionSpec as P

HEAD = 128
HEADS = 16
GROUP = 128
WIDTH = HEAD * HEADS
NZ, NX, NC, NY = 8, 4, 2, 4
F32 = jnp.float32
BF16 = jnp.bfloat16


def dot(a, b, contract):
    return lax.dot_general(
        a, b, (((contract[0],), (contract[1],)), ((), ())), preferred_element_type=F32
    )


def causal_mask():
    rows = lax.broadcasted_iota(jnp.int32, (GROUP, GROUP), 0)
    cols = lax.broadcasted_iota(jnp.int32, (GROUP, GROUP), 1)
    return rows >= cols


def columns(offsets, p):
    return pl.ds(pl.multiple_of(offsets[p], HEAD), HEAD)


def split_state(state):
    high = state.astype(BF16)
    low = (state - high.astype(F32)).astype(BF16)
    return high, low


def outer_kernel(offsets, k_ref, v_ref, keep_ref, send_ref):
    for p in range(HEADS):
        at = columns(offsets, p)
        out = keep_ref if p < 8 else send_ref
        out[p % 8] = dot(k_ref[:, at], v_ref[:, at], (0, 0))


def local_kernel(offsets, q_ref, k_ref, v_ref, weights_ref, attended_ref):
    causal = causal_mask()
    for p in range(HEADS):
        at = columns(offsets, p)
        scores = dot(q_ref[:, at], k_ref[:, at], (1, 1))
        weights = jnp.where(causal, scores, 0.0).astype(BF16)
        weights_ref[p] = weights
        attended_ref[p] = dot(weights, v_ref[:, at], (1, 0))


def norm_kernel(
    offsets, q_ref, g_ref, gain_ref, attended_ref, own_ref, other_ref,
    normed_ref, grad_ref, keep_ref, send_ref, gain_grad_ref,
):
    for p in range(HEADS):
        at = columns(offsets, p)
        query = q_ref[:, at]
        high, low = split_state((own_ref if p < 8 else other_ref)[p % 8])
        attended = attended_ref[p] + dot(query, high, (1, 0)) + dot(query, low, (1, 0))
        inv_rms = lax.rsqrt(jnp.mean(attended * attended, axis=1, keepdims=True) + 1e-05)
        normed = attended * inv_rms
        gain = gain_ref[:, at]
        normed_ref[:, at] = (normed * gain).astype(BF16)
        grad_wide = g_ref[:, at].astype(F32)
        grad_normed = grad_wide * gain
        gain_grad_ref[:, at] = jnp.sum(normed * grad_wide, axis=0, keepdims=True)
        grad_out = inv_rms * (
            grad_normed - normed * jnp.mean(grad_normed * normed, axis=1, keepdims=True)
        )
        grad_half = grad_out.astype(BF16)
        grad_ref[p] = grad_half
        (keep_ref if p < 8 else send_ref)[p % 8] = dot(query, grad_half, (0, 0))


def query_kernel(
    offsets, q_ref, k_ref, v_ref, grad_ref, weights_ref, own_ref, other_ref,
    query_grad_ref, key_part_ref, value_part_ref,
):
    causal = causal_mask()
    for p in range(HEADS):
        at = columns(offsets, p)
        grad_half = grad_ref[p]
        mixed = jnp.where(causal, dot(grad_half, v_ref[:, at], (1, 1)), 0.0).astype(BF16)
        high, low = split_state((own_ref if p < 8 else other_ref)[p % 8])
        query_grad_ref[:, at] = (
            dot(mixed, k_ref[:, at], (1, 0))
            + dot(grad_half, high, (1, 1))
            + dot(grad_half, low, (1, 1))
        ).astype(BF16)
        key_part_ref[p] = dot(mixed, q_ref[:, at], (0, 0))
        value_part_ref[p] = dot(weights_ref[p], grad_half, (0, 0))


def key_kernel(
    offsets, k_ref, v_ref, key_part_ref, value_part_ref, own_ref, other_ref,
    key_grad_ref, value_grad_ref,
):
    for p in range(HEADS):
        at = columns(offsets, p)
        high, low = split_state((own_ref if p < 8 else other_ref)[p % 8])
        value, key = v_ref[:, at], k_ref[:, at]
        key_grad_ref[:, at] = (
            key_part_ref[p] + dot(value, high, (1, 1)) + dot(value, low, (1, 1))
        ).astype(BF16)
        value_grad_ref[:, at] = (
            value_part_ref[p] + dot(key, high, (1, 0)) + dot(key, low, (1, 0))
        ).astype(BF16)


ROWS16 = jax.ShapeDtypeStruct((GROUP, WIDTH), BF16)
HALF = jax.ShapeDtypeStruct((8, HEAD, HEAD), F32)
FULL = jax.ShapeDtypeStruct((HEADS, GROUP, HEAD), F32)
FULL16 = jax.ShapeDtypeStruct((HEADS, GROUP, HEAD), BF16)


def call(kernel, outs, flops, *args):
    vmem = pl.BlockSpec(memory_space=pltpu.VMEM)
    moved = sum(a.size * a.dtype.itemsize for a in args)
    return pl.pallas_call(
        kernel,
        out_shape=outs,
        in_specs=[pl.BlockSpec(memory_space=pltpu.SMEM)] + [vmem] * (len(args) - 1),
        out_specs=[vmem] * len(outs),
        compiler_params=pltpu.CompilerParams(vmem_limit_bytes=24 << 20),
        cost_estimate=pl.CostEstimate(flops=flops, bytes_accessed=moved, transcendentals=0),
    )(*args)


MATMUL = 2 * HEADS * 128**3


def along_z(first):
    pairs = []
    for z in range(NZ):
        for c in range(NC):
            m = (z - c) % NZ
            even = m % 2 == 0
            step = 1 if even == first else -1
            pairs.append((z * NC + c, ((z + step) % NZ) * NC + c))
    return pairs


def z_sum(total, reverse):
    z, c = lax.axis_index("z"), lax.axis_index("core")
    m = (z - c) % NZ
    even = m % 2 == 0
    pair = m // 2
    partner = (z + jnp.where(even, 1, -1)) % NZ
    skipped = 0 if reverse else NZ - 1

    def needed(j):
        j = j % 4
        wrapped = (j == 3) & (c == 1)
        if reverse:
            return jnp.where(wrapped, NZ - 1, 2 * j + 1 + c) > z
        return jnp.where(wrapped, 0, 2 * j + c) < z

    def pick(flag, value):
        return jnp.where(flag, value, 0.0)

    swap_a = lambda v: lax.ppermute(v, ("z", "core"), along_z(True))
    swap_b = lambda v: lax.ppermute(v, ("z", "core"), along_z(False))
    mate = swap_a(total)
    both = pick(z != skipped, total) + pick(partner != skipped, mate)
    second = swap_b(both)
    third = swap_a(second)
    fourth = swap_b(third)
    side = jnp.where(even, -1, 1)
    base = pick((partner > z) if reverse else (partner < z), mate)
    base = base + pick(needed(pair + side), second)
    base = base + pick(needed(pair - side), third)
    return base + pick(needed(pair + 2), fourth)


def device_sum(keep, send, reverse):
    x, c = lax.axis_index("x"), lax.axis_index("core")
    swap = [(0, 1), (1, 0)]
    got = lax.ppermute(send, "core", swap)
    total = (keep + got).reshape(NX, 2, HEAD, HEAD)

    def shifted(value, s):
        return lax.ppermute(value, "x", [(i, (i + s) % NX) for i in range(NX)])

    parts = {0: total[0]}
    for s in (2, 1, 3):
        parts[s] = shifted(total[s], s)
    base = z_sum(parts[0] + parts[1] + parts[2] + parts[3], reverse)

    def chip_sum(s):
        target = (x + s) % NX
        value = base
        for t in range(NX):
            source = (x - t) % NX
            flag = (source > target) if reverse else (source < target)
            value = value + jnp.where(flag, parts[t], 0.0)
        return value

    slots = {0: chip_sum(0)}
    for s in (2, 1, 3):
        slots[(NX - s) % NX] = shifted(chip_sum(s), s)
    chip = jnp.concatenate([slots[s] for s in range(NX)], axis=0)
    mine = (c == 0) if reverse else (c == 1)
    own = chip + jnp.where(mine, got, 0.0)
    other = lax.ppermute(chip + jnp.where(mine, 0.0, keep), "core", swap)
    return own, other


def total_of(part):
    for axis, size in (("core", NC), ("dp", NY), ("x", NX)):
        for flip in (1,) if size == 2 else (1, 3):
            part = part + lax.ppermute(part, axis, [(i, i ^ flip) for i in range(size)])
    for flip in (1, 2, 4):
        part = part + lax.ppermute(part, "z", [(i, i ^ flip) for i in range(NZ)])
    return part


def per_device(queries, keys, values, out_grad, gain):
    q, k, v, g = (a.reshape(GROUP, WIDTH) for a in (queries, keys, values, out_grad))
    x, c = lax.axis_index("x"), lax.axis_index("core")
    p = jnp.arange(HEADS, dtype=jnp.int32)
    head = (c ^ (p // 8)) * 8 + ((x + (p % 8) // 2) % NX) * 2 + p % 2
    offsets = (head * HEAD).astype(jnp.int32)

    keep, send = call(outer_kernel, [HALF, HALF], MATMUL, offsets, k, v)
    weights, attended = call(local_kernel, [FULL16, FULL], 2 * MATMUL, offsets, q, k, v)
    own, other = device_sum(keep, send, False)
    normed_out, grad_half, keep, send, gain_part = call(
        norm_kernel,
        [ROWS16, FULL16, HALF, HALF, jax.ShapeDtypeStruct((1, WIDTH), F32)],
        3 * MATMUL,
        offsets, q, g, gain.reshape(1, WIDTH), attended, own, other,
    )
    query_grad, key_part, value_part = call(
        query_kernel, [ROWS16, FULL, FULL], 6 * MATMUL,
        offsets, q, k, v, grad_half, weights, own, other,
    )
    own, other = device_sum(keep, send, True)
    key_grad, value_grad = call(
        key_kernel, [ROWS16, ROWS16], 4 * MATMUL,
        offsets, k, v, key_part, value_part, own, other,
    )
    tokens = GROUP * NZ * NX * NC * NY
    gain_grad = total_of(gain_part.reshape(HEADS, HEAD)) / math.sqrt(tokens)
    shape = queries.shape
    return (
        normed_out.reshape(shape),
        query_grad.reshape(shape),
        key_grad.reshape(shape),
        value_grad.reshape(shape),
        gain_grad.reshape(WIDTH),
    )


def solution(mesh):
    fine = Mesh(mesh.devices.reshape(NZ, NX, NC, NY), ("z", "x", "core", "dp"))
    rows = P("dp", ("z", "x", "core"), None)
    return jax.shard_map(
        per_device,
        mesh=fine,
        in_specs=(rows, rows, rows, rows, P()),
        out_specs=(rows, rows, rows, rows, P()),
        check_vma=False,
    )
```

```python
import math

import jax
import jax.numpy as jnp
from jax import lax
from jax.experimental import pallas as pl
from jax.experimental.pallas import tpu as pltpu
from jax.sharding import Mesh, PartitionSpec as P

HEAD = 128
HEADS = 16
GROUP = 128
WIDTH = HEAD * HEADS
NZ, NX, NC, NY = 8, 4, 2, 4
F32 = jnp.float32
BF16 = jnp.bfloat16


def dot(a, b, contract):
    return lax.dot_general(
        a, b, (((contract[0],), (contract[1],)), ((), ())), preferred_element_type=F32
    )


def causal_mask():
    rows = lax.broadcasted_iota(jnp.int32, (GROUP, GROUP), 0)
    cols = lax.broadcasted_iota(jnp.int32, (GROUP, GROUP), 1)
    return rows >= cols


def columns(offsets, p):
    return pl.ds(pl.multiple_of(offsets[p], HEAD), HEAD)


def split_state(state):
    high = state.astype(BF16)
    low = (state - high.astype(F32)).astype(BF16)
    return high, low


def outer_kernel(offsets, k_ref, v_ref, keep_ref, send_ref):
    for p in range(HEADS):
        at = columns(offsets, p)
        out = keep_ref if p < 8 else send_ref
        out[p % 8] = dot(k_ref[:, at], v_ref[:, at], (0, 0))


def local_kernel(offsets, q_ref, k_ref, v_ref, weights_ref, attended_ref):
    causal = causal_mask()
    for p in range(HEADS):
        at = columns(offsets, p)
        scores = dot(q_ref[:, at], k_ref[:, at], (1, 1))
        weights = jnp.where(causal, scores, 0.0).astype(BF16)
        weights_ref[p] = weights
        attended_ref[p] = dot(weights, v_ref[:, at], (1, 0))


def norm_kernel(
    offsets, q_ref, g_ref, gain_ref, attended_ref, own_ref, other_ref,
    normed_ref, grad_ref, keep_ref, send_ref, gain_grad_ref,
):
    for p in range(HEADS):
        at = columns(offsets, p)
        query = q_ref[:, at]
        high, low = split_state((own_ref if p < 8 else other_ref)[p % 8])
        attended = attended_ref[p] + dot(query, high, (1, 0)) + dot(query, low, (1, 0))
        inv_rms = lax.rsqrt(jnp.mean(attended * attended, axis=1, keepdims=True) + 1e-05)
        normed = attended * inv_rms
        gain = gain_ref[:, at]
        normed_ref[:, at] = (normed * gain).astype(BF16)
        grad_wide = g_ref[:, at].astype(F32)
        grad_normed = grad_wide * gain
        gain_grad_ref[:, at] = jnp.sum(normed * grad_wide, axis=0, keepdims=True)
        grad_out = inv_rms * (
            grad_normed - normed * jnp.mean(grad_normed * normed, axis=1, keepdims=True)
        )
        grad_half = grad_out.astype(BF16)
        grad_ref[p] = grad_half
        (keep_ref if p < 8 else send_ref)[p % 8] = dot(query, grad_half, (0, 0))


def query_kernel(
    offsets, q_ref, k_ref, v_ref, grad_ref, weights_ref, own_ref, other_ref,
    query_grad_ref, key_part_ref, value_part_ref,
):
    causal = causal_mask()
    for p in range(HEADS):
        at = columns(offsets, p)
        grad_half = grad_ref[p]
        mixed = jnp.where(causal, dot(grad_half, v_ref[:, at], (1, 1)), 0.0).astype(BF16)
        high, low = split_state((own_ref if p < 8 else other_ref)[p % 8])
        query_grad_ref[:, at] = (
            dot(mixed, k_ref[:, at], (1, 0))
            + dot(grad_half, high, (1, 1))
            + dot(grad_half, low, (1, 1))
        ).astype(BF16)
        key_part_ref[p] = dot(mixed, q_ref[:, at], (0, 0))
        value_part_ref[p] = dot(weights_ref[p], grad_half, (0, 0))


def key_kernel(
    offsets, k_ref, v_ref, key_part_ref, value_part_ref, own_ref, other_ref,
    key_grad_ref, value_grad_ref,
):
    for p in range(HEADS):
        at = columns(offsets, p)
        high, low = split_state((own_ref if p < 8 else other_ref)[p % 8])
        value, key = v_ref[:, at], k_ref[:, at]
        key_grad_ref[:, at] = (
            key_part_ref[p] + dot(value, high, (1, 1)) + dot(value, low, (1, 1))
        ).astype(BF16)
        value_grad_ref[:, at] = (
            value_part_ref[p] + dot(key, high, (1, 0)) + dot(key, low, (1, 0))
        ).astype(BF16)


ROWS16 = jax.ShapeDtypeStruct((GROUP, WIDTH), BF16)
HALF = jax.ShapeDtypeStruct((8, HEAD, HEAD), F32)
FULL = jax.ShapeDtypeStruct((HEADS, GROUP, HEAD), F32)
FULL16 = jax.ShapeDtypeStruct((HEADS, GROUP, HEAD), BF16)


def call(kernel, outs, flops, *args):
    vmem = pl.BlockSpec(memory_space=pltpu.VMEM)
    moved = sum(a.size * a.dtype.itemsize for a in args)
    return pl.pallas_call(
        kernel,
        out_shape=outs,
        in_specs=[pl.BlockSpec(memory_space=pltpu.SMEM)] + [vmem] * (len(args) - 1),
        out_specs=[vmem] * len(outs),
        compiler_params=pltpu.CompilerParams(vmem_limit_bytes=8 << 20),
        cost_estimate=pl.CostEstimate(flops=flops, bytes_accessed=moved, transcendentals=0),
    )(*args)


MATMUL = 2 * HEADS * 128**3


def z_pairs(moves, reverse):
    at = (lambda y: NZ - 1 - y) if reverse else (lambda y: y)
    return [(at(a), at(b)) for a, b in moves]


UP_ONE = [(y, y + 1) for y in range(7)]
DOWN_ONE = [(0, 7), (1, 0), (2, 1), (3, 2), (4, 3), (5, 4)]
UP_THREE = [(0, 3), (1, 4), (2, 5), (3, 6), (4, 7), (7, 2)]
DOWN_TWO = [(7, 5), (0, 6), (1, 7)]


def tie(*values):
    return lax.optimization_barrier(values)


def flag_rows(z, x, c):
    row = lax.broadcasted_iota(jnp.int32, (40, HEAD), 0)
    slot, step = (row >> 2) & 3, row & 3
    source, target = (x - step) & 3, (x + slot) & 3
    flag = jnp.where(row < 16, source < target, source > target)
    flag = jnp.where(row == 32, z == NZ - 1, flag)
    flag = jnp.where(row == 33, z == 0, flag)
    flag = jnp.where(row == 34, c == 1, flag)
    flag = jnp.where(row == 35, c == 0, flag)
    return flag.astype(F32)


def shift_x(value, s):
    return lax.ppermute(value, "x", [(i, (i + s) % NX) for i in range(NX)])


def swap_cores(value):
    return lax.ppermute(value, "core", [(0, 1), (1, 0)])


def device_sum(keep, send, flags, reverse, beside):
    def flag(row):
        return flags[row].reshape(1, 1, HEAD)

    last = flag(33 if reverse else 32)
    mine = flag(35 if reverse else 34)

    def move(value, moves):
        return lax.ppermute(value, "z", z_pairs(moves, reverse))

    got = swap_cores(send)
    (got,) = beside("core", got)
    total = (keep + got).reshape(NX, 2, HEAD, HEAD)
    third, second, first = (shift_x(total[s], s) for s in (3, 2, 1))
    first, second, third = beside("x", first, second, third)
    parts = (total[0], first, second, third)
    whole = (parts[0] + parts[1]) + (parts[2] + parts[3])

    below, above = move(whole, UP_ONE), move(whole, DOWN_ONE)
    below, above = beside("z1", below, above)
    pair = (1.0 - last) * whole + above
    three = move(pair + (1.0 - last) * below, UP_THREE)
    two = move(pair, DOWN_TWO)
    three, two = beside("z2", three, two)
    base = (below + last * above) + (three + two)

    def chip_sum(s):
        value = base
        for t in range(NX):
            value = value + flag((16 if reverse else 0) + 4 * s + t) * parts[t]
        return value

    third, second, first = (shift_x(chip_sum(s), s) for s in (3, 2, 1))
    first, second, third = beside("back", first, second, third)
    chip = jnp.concatenate([chip_sum(0), third, second, first], axis=0)
    other = swap_cores(chip + (1.0 - mine) * keep)
    return chip + mine * got, other


def flip_sum(part, axis, flip):
    size = {"core": NC, "dp": NY, "x": NX, "z": NZ}[axis]
    return part + lax.ppermute(part, axis, [(i, i ^ flip) for i in range(size)])


def per_device(queries, keys, values, out_grad, gain):
    q, k, v, g = (a.reshape(GROUP, WIDTH) for a in (queries, keys, values, out_grad))
    z, x, c = (lax.axis_index(name) for name in ("z", "x", "core"))
    p = jnp.arange(HEADS, dtype=jnp.int32)
    head = (c ^ (p // 8)) * 8 + ((x + (p % 8) // 2) & 3) * 2 + p % 2
    offsets, flags = tie((head * HEAD).astype(jnp.int32), flag_rows(z, x, c))

    local = []

    def beside_first(stage, *values):
        if stage != "z1":
            return values
        local.extend(call(local_kernel, [FULL16, FULL], 2 * MATMUL, offsets, q, k, v))
        return tie(*values, *local)[: len(values)]

    keep, send = call(outer_kernel, [HALF, HALF], MATMUL, offsets, k, v)
    own, other = device_sum(keep, send, flags, False, beside_first)
    weights, attended = local
    normed_out, grad_half, keep, send, gain_part = call(
        norm_kernel,
        [ROWS16, FULL16, HALF, HALF, jax.ShapeDtypeStruct((1, WIDTH), F32)],
        3 * MATMUL,
        offsets, q, g, gain.reshape(1, WIDTH), attended, own, other,
    )
    side = {"gain": gain_part.reshape(HEADS, HEAD)}
    flips = {
        "core": [("core", 1)],
        "x": [("dp", 1), ("dp", 3)],
        "z1": [("x", 1)],
        "z2": [("x", 3)],
        "back": [("z", 1), ("z", 2)],
    }

    def beside_second(stage, *values):
        part = side["gain"]
        for axis, flip in flips[stage]:
            part = flip_sum(part, axis, flip)
        extra = [part]
        if stage == "z2":
            query = call(
                query_kernel, [ROWS16, FULL, FULL], 6 * MATMUL,
                offsets, q, k, v, grad_half, weights, own, other,
            )
            extra.extend(query)
        tied = tie(*values, *extra)
        side["gain"] = tied[len(values)]
        if stage == "z2":
            side["query"] = tied[len(values) + 1 :]
        return tied[: len(values)]

    after_own, after_other = device_sum(keep, send, flags, True, beside_second)
    query_grad, key_part, value_part = side["query"]
    key_grad, value_grad = call(
        key_kernel, [ROWS16, ROWS16], 4 * MATMUL,
        offsets, k, v, key_part, value_part, after_own, after_other,
    )
    tokens = GROUP * NZ * NX * NC * NY
    gain_grad = flip_sum(side["gain"], "z", 4) / math.sqrt(tokens)
    shape = queries.shape
    return (
        normed_out.reshape(shape),
        query_grad.reshape(shape),
        key_grad.reshape(shape),
        value_grad.reshape(shape),
        gain_grad.reshape(WIDTH),
    )


def solution(mesh):
    fine = Mesh(mesh.devices.reshape(NZ, NX, NC, NY), ("z", "x", "core", "dp"))
    rows = P("dp", ("z", "x", "core"), None)
    return jax.shard_map(
        per_device,
        mesh=fine,
        in_specs=(rows, rows, rows, rows, P()),
        out_specs=(rows, rows, rows, rows, P()),
        check_vma=False,
    )
```

```python
import math

import jax
import jax.numpy as jnp
from jax import lax
from jax.experimental import pallas as pl
from jax.experimental.pallas import tpu as pltpu
from jax.sharding import Mesh, PartitionSpec as P

HEAD = 128
HEADS = 16
GROUP = 128
WIDTH = HEAD * HEADS
NZ, NX, NC, NY = 8, 4, 2, 4
F32 = jnp.float32
BF16 = jnp.bfloat16
TOKENS = GROUP * NZ * NX * NC * NY


def dot(a, b, contract):
    return lax.dot_general(
        a, b, (((contract[0],), (contract[1],)), ((), ())), preferred_element_type=F32
    )


def causal_mask():
    rows = lax.broadcasted_iota(jnp.int32, (GROUP, GROUP), 0)
    cols = lax.broadcasted_iota(jnp.int32, (GROUP, GROUP), 1)
    return rows >= cols


def columns(offsets, p):
    return pl.ds(pl.multiple_of(offsets[p], HEAD), HEAD)


def split_state(state):
    high = state.astype(BF16)
    low = (state - high.astype(F32)).astype(BF16)
    return high, low


def outer_kernel(offsets, k_ref, v_ref, keep_ref, send_ref):
    for p in range(HEADS):
        at = columns(offsets, p)
        out = keep_ref if p < 8 else send_ref
        out[p % 8] = dot(k_ref[:, at], v_ref[:, at], (0, 0))


def local_kernel(offsets, q_ref, k_ref, v_ref, weights_ref, attended_ref):
    causal = causal_mask()
    for p in range(HEADS):
        at = columns(offsets, p)
        scores = dot(q_ref[:, at], k_ref[:, at], (1, 1))
        weights = jnp.where(causal, scores, 0.0).astype(BF16)
        weights_ref[p] = weights
        attended_ref[p] = dot(weights, v_ref[:, at], (1, 0))


def norm_kernel(
    offsets, q_ref, g_ref, gain_ref, attended_ref, own_ref, other_ref,
    normed_ref, grad_ref, keep_ref, send_ref, gain_grad_ref,
):
    gain_grad_ref[...] = jnp.zeros_like(gain_grad_ref)
    for p in range(HEADS):
        at = columns(offsets, p)
        query = q_ref[:, at]
        high, low = split_state((own_ref if p < 8 else other_ref)[p % 8])
        attended = attended_ref[p] + dot(query, high, (1, 0)) + dot(query, low, (1, 0))
        inv_rms = lax.rsqrt(jnp.mean(attended * attended, axis=1, keepdims=True) + 1e-05)
        normed = attended * inv_rms
        gain = gain_ref[:, at]
        normed_ref[:, at] = (normed * gain).astype(BF16)
        grad_wide = g_ref[:, at].astype(F32)
        grad_normed = grad_wide * gain
        row = 2 * (p // 8) + p % 2
        gain_grad_ref[(p % 8) // 2, row : row + 1] = jnp.sum(normed * grad_wide, axis=0, keepdims=True)
        grad_out = inv_rms * (
            grad_normed - normed * jnp.mean(grad_normed * normed, axis=1, keepdims=True)
        )
        grad_half = grad_out.astype(BF16)
        grad_ref[p] = grad_half
        (keep_ref if p < 8 else send_ref)[p % 8] = dot(query, grad_half, (0, 0))


def query_kernel(
    offsets, q_ref, k_ref, v_ref, grad_ref, weights_ref, own_ref, other_ref,
    query_grad_ref, key_part_ref, value_part_ref,
):
    causal = causal_mask()
    for p in range(HEADS):
        at = columns(offsets, p)
        grad_half = grad_ref[p]
        mixed = jnp.where(causal, dot(grad_half, v_ref[:, at], (1, 1)), 0.0).astype(BF16)
        high, low = split_state((own_ref if p < 8 else other_ref)[p % 8])
        query_grad_ref[:, at] = (
            dot(mixed, k_ref[:, at], (1, 0))
            + dot(grad_half, high, (1, 1))
            + dot(grad_half, low, (1, 1))
        ).astype(BF16)
        key_part_ref[p] = dot(mixed, q_ref[:, at], (0, 0))
        value_part_ref[p] = dot(weights_ref[p], grad_half, (0, 0))


def key_kernel(
    offsets, k_ref, v_ref, key_part_ref, value_part_ref, own_ref, other_ref,
    key_grad_ref, value_grad_ref,
):
    for p in range(HEADS):
        at = columns(offsets, p)
        high, low = split_state((own_ref if p < 8 else other_ref)[p % 8])
        value, key = v_ref[:, at], k_ref[:, at]
        key_grad_ref[:, at] = (
            key_part_ref[p] + dot(value, high, (1, 1)) + dot(value, low, (1, 1))
        ).astype(BF16)
        value_grad_ref[:, at] = (
            value_part_ref[p] + dot(key, high, (1, 0)) + dot(key, low, (1, 0))
        ).astype(BF16)


GAIN_TERMS = ((0, 0), (8, -1), (16, 1), (24, -3), (28, -4), (32, -2), (40, 2), (44, 3))


def gain_kernel(place, terms_ref, out_ref, by_place):
    for row, further in GAIN_TERMS:
        by_place[(place[0] + further + NZ) & (NZ - 1)] = terms_ref[row : row + 4]
    total = by_place[0]
    for y in range(1, NZ):
        total = total + by_place[y]
    out_ref[0:4] = total
    out_ref[4:8] = jnp.zeros_like(total)


def scale_kernel(offsets, rows_ref, out_ref):
    for p in range(HEADS):
        out_ref[:, columns(offsets, p)] = rows_ref[p : p + 1] / math.sqrt(TOKENS)


ROWS16 = jax.ShapeDtypeStruct((GROUP, WIDTH), BF16)
HALF = jax.ShapeDtypeStruct((8, HEAD, HEAD), F32)
FULL = jax.ShapeDtypeStruct((HEADS, GROUP, HEAD), F32)
FULL16 = jax.ShapeDtypeStruct((HEADS, GROUP, HEAD), BF16)


def call(kernel, outs, flops, *args, scratch=()):
    vmem = pl.BlockSpec(memory_space=pltpu.VMEM)
    moved = sum(a.size * a.dtype.itemsize for a in args)
    return pl.pallas_call(
        kernel,
        out_shape=outs,
        in_specs=[pl.BlockSpec(memory_space=pltpu.SMEM)] + [vmem] * (len(args) - 1),
        out_specs=[vmem] * len(outs),
        scratch_shapes=list(scratch),
        compiler_params=pltpu.CompilerParams(vmem_limit_bytes=8 << 20),
        cost_estimate=pl.CostEstimate(flops=flops, bytes_accessed=moved, transcendentals=0),
    )(*args)


MATMUL = 2 * HEADS * 128**3


def tie(*values):
    return lax.optimization_barrier(values)


def flag_rows(z, x, c):
    row = lax.broadcasted_iota(jnp.int32, (48, HEAD), 0)
    slot, step = (row >> 2) & 3, row & 3
    source, target = (x - step) & 3, (x + slot) & 3
    flag = jnp.where(row < 16, source < target, source > target)
    kind = row & 7
    y = jnp.where(row < 40, z, NZ - 1 - z)
    core = jnp.where(row < 40, c == 1, c == 0)
    along = (y >= 1) & ((kind != 1) | (y < NZ - 1))
    along = jnp.where(kind == 2, y == NZ - 1, along)
    along = jnp.where(kind == 3, y >= 2, along)
    along = jnp.where(kind == 4, y >= 5, along)
    along = jnp.where(kind == 5, core, along)
    return jnp.where(row < 32, flag, along).astype(F32)


def shift(value, axis, s):
    size = lax.axis_size(axis)
    return lax.ppermute(value, axis, [(i, (i + s) % size) for i in range(size)])


def flip(value, axis, bits):
    return lax.ppermute(value, axis, [(i, i ^ bits) for i in range(lax.axis_size(axis))])


MAIN = 2 * HEAD


def join(main, *rows):
    return jnp.concatenate([main, *rows], axis=0) if rows else main


def device_sum(keep, send, flags, reverse, beside, gain=None, place=None):
    def flag(row):
        return flags[row].reshape(1, HEAD)

    z_row = 40 if reverse else 32
    has_below, inner, last, from_two, from_five, mine = (flag(z_row + i) for i in range(6))

    def along(value, places):
        return shift(value, "z", -places if reverse else places)

    keep = keep.reshape(NX, MAIN, HEAD)
    got = swapped = flip(send.reshape(NX, MAIN, HEAD), "core", 1)
    if gain is not None:
        got, gain = tie(swapped, gain + flip(gain, "dp", 1))
    rows = [() if gain is None else (gain[s],) for s in range(NX)]
    total = [join(keep[s] + got[s], *rows[s]) for s in range(NX)]
    third, second, first = (shift(total[s], "x", s) for s in (3, 2, 1))
    first, second, third = beside("x", total[0], first, second, third)
    parts = (total[0], first, second, third)
    whole = (parts[0] + parts[1]) + (parts[2] + parts[3])

    below, above = tie(along(whole, 1), along(whole, -1))
    heads, heads_below, heads_above = whole[:MAIN], below[:MAIN], above[:MAIN]
    pair = (1.0 - last) * heads + heads_above
    triple = pair + inner * heads_below
    if gain is not None:
        a, b, c = (v[MAIN : MAIN + 4] for v in (whole, below, above))
        triple, pair = join(triple, a, b, c, c), join(pair, a, c)
    three, two = tie(along(triple, 3), along(pair, -2))
    base = (has_below * heads_below + last * heads_above) + (
        from_two * three[:MAIN] + from_five * two[:MAIN]
    )
    rows = ()
    if gain is not None:
        terms = jnp.concatenate([v[MAIN:] for v in (whole, below, above, three, two)], axis=0)
        rows = call(
            gain_kernel, [jax.ShapeDtypeStruct((8, HEAD), F32)], 0, place, terms,
            scratch=[pltpu.VMEM((NZ, 4, HEAD), F32)],
        )

    def chip_sum(s):
        value = base
        for t in range(NX):
            value = value + flag((16 if reverse else 0) + 4 * s + t) * parts[t][:MAIN]
        return join(value, *rows)

    third, second, first = (shift(chip_sum(s), "x", s) for s in (3, 2, 1))
    first, second, third = tie(first, second, third)
    slots = (chip_sum(0), third, second, first)
    chip = jnp.stack([v[:MAIN] for v in slots])
    own = (chip + mine * got).reshape(8, HEAD, HEAD)
    other = flip(chip + (1.0 - mine) * keep, "core", 1).reshape(8, HEAD, HEAD)
    if gain is None:
        return own, other
    rows = jnp.concatenate([v[MAIN + 2 * i : MAIN + 2 * i + 2] for i in (0, 1) for v in slots])
    return own, other, rows


def per_device(queries, keys, values, out_grad, gain):
    q, k, v, g = (a.reshape(GROUP, WIDTH) for a in (queries, keys, values, out_grad))
    z, x, c = (lax.axis_index(name) for name in ("z", "x", "core"))
    p = jnp.arange(HEADS, dtype=jnp.int32)
    head = (c ^ (p // 8)) * 8 + ((x + (p % 8) // 2) & 3) * 2 + p % 2
    place = jnp.broadcast_to(NZ - 1 - z, (1,)).astype(jnp.int32)
    offsets, flags, place = tie((head * HEAD).astype(jnp.int32), flag_rows(z, x, c), place)

    local = []

    def beside_first(stage, ready, *values):
        queries, _ = tie(q, ready)
        local.extend(call(local_kernel, [FULL16, FULL], 2 * MATMUL, offsets, queries, k, v))
        return tie(*values, *local)[: len(values)]

    keep, send = call(outer_kernel, [HALF, HALF], MATMUL, offsets, k, v)
    own, other = device_sum(keep, send, flags, False, beside_first)
    weights, attended = local
    normed_out, grad_half, keep, send, gain_part = call(
        norm_kernel,
        [ROWS16, FULL16, HALF, HALF, jax.ShapeDtypeStruct((NX, 8, HEAD), F32)],
        3 * MATMUL,
        offsets, q, g, gain.reshape(1, WIDTH), attended, own, other,
    )
    query = []

    def beside_second(stage, ready, *values):
        queries, _ = tie(q, ready)
        query.extend(
            call(
                query_kernel, [ROWS16, FULL, FULL], 6 * MATMUL,
                offsets, queries, k, v, grad_half, weights, own, other,
            )
        )
        return tie(*values, *query)[: len(values)]

    after_own, after_other, rows = device_sum(
        keep, send, flags, True, beside_second, gain_part, place
    )
    rows = rows + flip(rows, "dp", 3)
    rows, after_own, after_other = tie(rows, after_own, after_other)
    crossed = flip(rows, "core", 1)
    query_grad, key_part, value_part = query
    key_grad, value_grad = call(
        key_kernel, [ROWS16, ROWS16], 4 * MATMUL,
        offsets, k, v, key_part, value_part, after_own, after_other,
    )
    rows = rows + jnp.concatenate([crossed[8:], crossed[:8]])
    (gain_grad,) = call(scale_kernel, [jax.ShapeDtypeStruct((1, WIDTH), F32)], 0, offsets, rows)
    shape = queries.shape
    return (
        normed_out.reshape(shape),
        query_grad.reshape(shape),
        key_grad.reshape(shape),
        value_grad.reshape(shape),
        gain_grad.reshape(WIDTH),
    )


def solution(mesh):
    fine = Mesh(mesh.devices.reshape(NZ, NX, NC, NY), ("z", "x", "core", "dp"))
    rows = P("dp", ("z", "x", "core"), None)
    return jax.shard_map(
        per_device,
        mesh=fine,
        in_specs=(rows, rows, rows, rows, P()),
        out_specs=(rows, rows, rows, rows, P()),
        check_vma=False,
    )
```

```python
import functools
import math

import jax
import jax.numpy as jnp
from jax import lax
from jax.experimental import pallas as pl
from jax.experimental.pallas import tpu as pltpu
from jax.sharding import Mesh, PartitionSpec as P

HEAD = 128
HEADS = 16
GROUP = 128
WIDTH = HEAD * HEADS
NZ, NX, NC, NY = 8, 4, 2, 4
TOKENS = GROUP * NZ * NX * NC * NY
F32 = jnp.float32
BF16 = jnp.bfloat16


OWN = tuple(range(8))
OTHER = tuple(range(8, 16))
MAIN = 2 * HEAD
GAIN_TERMS = ((0, 0, 0), (1, 0, -1), (2, 0, 1), (3, 0, -3), (3, 4, -4), (3, 8, -2), (4, 0, 2), (4, 4, 3))


def dot(a, b, contract):
    return lax.dot_general(
        a, b, (((contract[0],), (contract[1],)), ((), ())), preferred_element_type=F32
    )


def causal_mask():
    rows = lax.broadcasted_iota(jnp.int32, (GROUP, GROUP), 0)
    cols = lax.broadcasted_iota(jnp.int32, (GROUP, GROUP), 1)
    return rows >= cols


def here():
    return lax.axis_index("z"), lax.axis_index("x"), lax.axis_index("core")


def first_column(p):
    _, x, c = here()
    head = (c ^ (p // 8)) * 8 + ((x + (p % 8) // 2) & 3) * 2 + p % 2
    return head * HEAD


def columns(p):
    return pl.ds(pl.multiple_of(first_column(p), HEAD), HEAD)


def split_state(state, axis):
    high = state.astype(BF16)
    low = (state - high.astype(F32)).astype(BF16)
    return jnp.concatenate([high, low], axis=axis)


def twice(value):
    return jnp.concatenate([value, value], axis=1)


def one_if(flag):
    return jnp.where(flag, 1.0, 0.0).astype(F32)


def send_kernel(k_hbm, v_hbm, out_ref, k_half, v_half, sems):
    first = pl.multiple_of((1 - here()[2]) * (WIDTH // 2), WIDTH // 2)
    half = pl.ds(first, WIDTH // 2)
    copies = (
        pltpu.make_async_copy(k_hbm.at[:, half], k_half, sems.at[0]),
        pltpu.make_async_copy(v_hbm.at[:, half], v_half, sems.at[1]),
    )
    for copy in copies:
        copy.start()
    for copy in copies:
        copy.wait()
    for p in OTHER:
        at = pl.ds(pl.multiple_of(first_column(p) - first, HEAD), HEAD)
        out_ref[p - 8] = dot(k_half[:, at], v_half[:, at], (0, 0))


def keep_kernel(k_ref, v_ref, out_ref):
    for p in OWN:
        at = columns(p)
        out_ref[p] = dot(k_ref[:, at], v_ref[:, at], (0, 0))


def local_kernel(q_ref, k_ref, v_ref, weights_ref, attended_ref):
    causal = causal_mask()
    for p in range(HEADS):
        at = columns(p)
        scores = dot(q_ref[:, at], k_ref[:, at], (1, 1))
        weights_ref[p] = jnp.where(causal, scores, 0.0).astype(BF16)
    for p in range(HEADS):
        attended_ref[p] = dot(weights_ref[p], v_ref[:, columns(p)], (1, 0))


def norm_rows(positions, q_ref, g_ref, gain_ref, local_ref, state_ref, first, normed_ref, grad_ref, attended_ref, store):
    for i, p in enumerate(positions):
        both = split_state(state_ref[p - first], 0)
        attended_ref[i] = local_ref[p] + dot(twice(q_ref[:, columns(p)]), both, (1, 0))
    for i, p in enumerate(positions):
        at = columns(p)
        attended = attended_ref[i]
        inv_rms = lax.rsqrt(jnp.mean(attended * attended, axis=1, keepdims=True) + 1e-05)
        normed = attended * inv_rms
        gain = gain_ref[:, at]
        normed_ref[i] = (normed * gain).astype(BF16)
        grad_wide = g_ref[:, at].astype(F32)
        product = normed * grad_wide
        store(i, jnp.sum(product, axis=0, keepdims=True))
        along = jnp.mean(product * gain, axis=1, keepdims=True)
        grad_ref[i] = (inv_rms * (grad_wide * gain - normed * along)).astype(BF16)


def own_norm_kernel(
    positions, first, q_ref, g_ref, gain_ref, local_ref, state_ref,
    normed_ref, grad_ref, sums_ref, attended_ref,
):
    def store(i, value):
        sums_ref[i : i + 1] = value

    norm_rows(positions, q_ref, g_ref, gain_ref, local_ref, state_ref, first, normed_ref, grad_ref, attended_ref, store)


def other_norm_kernel(
    q_ref, g_ref, gain_ref, local_ref, state_ref, sums_a_ref, sums_b_ref,
    normed_ref, grad_ref, send_ref, gain_rows_ref, attended_ref,
):
    def store(i, value):
        gain_rows_ref[i // 2, 2 + i % 2 : 3 + i % 2] = value

    norm_rows(OTHER, q_ref, g_ref, gain_ref, local_ref, state_ref, 8, normed_ref, grad_ref, attended_ref, store)
    for i, p in enumerate(OTHER):
        send_ref[i] = dot(q_ref[:, columns(p)], grad_ref[i], (0, 0))
    for s in range(NX):
        gain_rows_ref[s, 0:2] = sums_a_ref[...] if s == 0 else sums_b_ref[2 * s - 2 : 2 * s]
        gain_rows_ref[s, 4:8] = jnp.zeros((4, HEAD), F32)


def own_outer_kernel(q_ref, grad_a_ref, grad_b_ref, keep_ref):
    for p in OWN:
        grad = grad_a_ref[p] if p < 2 else grad_b_ref[p - 2]
        keep_ref[p] = dot(q_ref[:, columns(p)], grad, (0, 0))


def query_kernel(
    q_ref, k_ref, v_ref, weights_ref, own_ref, other_ref,
    grad_a_ref, grad_b_ref, grad_c_ref, normed_a_ref, normed_b_ref, normed_c_ref,
    normed_out_ref, query_grad_ref, key_part_ref, value_part_ref, mixed_ref,
):
    causal = causal_mask()

    def of(p, a_ref, b_ref, c_ref):
        return a_ref[p] if p < 2 else b_ref[p - 2] if p < 8 else c_ref[p - 8]

    def grad(p):
        return of(p, grad_a_ref, grad_b_ref, grad_c_ref)

    for p in range(HEADS):
        at = columns(p)
        normed_out_ref[:, at] = of(p, normed_a_ref, normed_b_ref, normed_c_ref)
        mixed_ref[p] = jnp.where(causal, dot(grad(p), v_ref[:, at], (1, 1)), 0.0).astype(BF16)
    for p in range(HEADS):
        at = columns(p)
        both = split_state((own_ref if p < 8 else other_ref)[p % 8], 1)
        query_grad_ref[:, at] = (
            dot(mixed_ref[p], k_ref[:, at], (1, 0)) + dot(twice(grad(p)), both, (1, 1))
        ).astype(BF16)
        key_part_ref[p] = dot(mixed_ref[p], q_ref[:, at], (0, 0))
        value_part_ref[p] = dot(weights_ref[p], grad(p), (0, 0))


def key_rows(p, k_ref, v_ref, key_part_ref, value_part_ref, state):
    at = columns(p)
    key = key_part_ref[p] + dot(twice(v_ref[:, at]), split_state(state, 1), (1, 1))
    value = value_part_ref[p] + dot(twice(k_ref[:, at]), split_state(state, 0), (1, 0))
    return key.astype(BF16), value.astype(BF16)


def own_key_kernel(k_ref, v_ref, key_part_ref, value_part_ref, state_ref, key_ref, value_ref):
    for p in OWN:
        key_ref[p], value_ref[p] = key_rows(
            p, k_ref, v_ref, key_part_ref, value_part_ref, state_ref[p]
        )


def other_key_kernel(
    k_ref, v_ref, key_part_ref, value_part_ref, state_ref, own_key_ref, own_value_ref,
    key_grad_ref, value_grad_ref,
):
    for p in OWN:
        at = columns(p)
        key_grad_ref[:, at] = own_key_ref[p]
        value_grad_ref[:, at] = own_value_ref[p]
    for p in OTHER:
        at = columns(p)
        key_grad_ref[:, at], value_grad_ref[:, at] = key_rows(
            p, k_ref, v_ref, key_part_ref, value_part_ref, state_ref[p - 8]
        )


def scale_kernel(rows_ref, out_ref):
    for p in range(HEADS):
        out_ref[:, columns(p)] = rows_ref[p : p + 1] / math.sqrt(TOKENS)


def along_scan(reverse):
    y = NZ - 1 - here()[0] if reverse else here()[0]
    return y, 1 - 2 * here()[2]


def total_kernel(with_gain, *refs):
    keep_ref, got_ref = refs[:2]
    outs = refs[-NX:]
    for s in range(NX):
        for j in range(2):
            outs[s][j * HEAD : (j + 1) * HEAD] = keep_ref[2 * s + j] + got_ref[2 * s + j]
        if with_gain:
            outs[s][MAIN : MAIN + 8] = refs[2][s] + refs[3][s]


def message_kernel(reverse, with_gain, whole_ref, behind_ref, ahead_ref, three_ref, two_ref):
    y, way = along_scan(reverse)
    further, back = (y + 3 * way) & 7, (y - 2 * way) & 7
    whole, behind, ahead = whole_ref[:MAIN], behind_ref[:MAIN], ahead_ref[:MAIN]
    before, after = (y - way) & 7, (y + way) & 7
    three_ref[:MAIN] = (
        one_if(y < further) * whole + one_if(before < further) * behind + one_if(after < further) * ahead
    )
    two_ref[:MAIN] = one_if(y < back) * whole + one_if(after < back) * ahead
    if with_gain:
        for i, ref in enumerate((whole_ref, behind_ref, ahead_ref)):
            three_ref[MAIN + 4 * i : MAIN + 4 * i + 4] = ref[MAIN : MAIN + 4]
        three_ref[MAIN + 12 : MAIN + 16] = jnp.zeros((4, HEAD), F32)
        for i, ref in enumerate((whole_ref, ahead_ref)):
            two_ref[MAIN + 4 * i : MAIN + 4 * i + 4] = ref[MAIN : MAIN + 4]


def chip_kernel(reverse, with_gain, *refs):
    whole_ref, behind_ref, ahead_ref, three_ref, two_ref = refs[:5]
    parts, got_ref = refs[5:9], refs[9]
    outs, own_ref = refs[10:14], refs[14]
    y, way = along_scan(reverse)
    base = (
        one_if(((y - way) & 7) < y) * behind_ref[:MAIN]
        + one_if(((y + way) & 7) < y) * ahead_ref[:MAIN]
        + (three_ref[:MAIN] + two_ref[:MAIN])
    )
    x = here()[1]
    for s in range(NX):
        value = base
        target = (x + s) & 3
        for t in range(NX):
            source = (x - t) & 3
            flag = source > target if reverse else source < target
            value = value + one_if(flag) * parts[t][:MAIN]
        outs[s][:MAIN] = value
        if s == 0 and not with_gain:
            mine = one_if(here()[2] == (0 if reverse else 1))
            for j in range(2):
                own_ref[j] = value[j * HEAD : (j + 1) * HEAD] + mine * got_ref[j]
    if with_gain:
        by_place = refs[14]
        for which, row, further in GAIN_TERMS:
            by_place[(y + further * way) & 7] = refs[which][MAIN + row : MAIN + row + 4]
        total = by_place[0]
        for i in range(1, NZ):
            total = total + by_place[i]
        for s in range(NX):
            outs[s][MAIN : MAIN + 4] = total
            outs[s][MAIN + 4 : MAIN + 8] = jnp.zeros_like(total)


def last_kernel(reverse, with_gain, *refs):
    slots, keep_ref, got_ref = refs[:NX], refs[NX], refs[NX + 1]
    own_ref, send_ref = refs[NX + 2], refs[NX + 3]
    mine = one_if(here()[2] == (0 if reverse else 1))
    for s in range(NX):
        for j in range(2):
            chip = slots[s][j * HEAD : (j + 1) * HEAD]
            own_ref[2 * s + j] = chip + mine * got_ref[2 * s + j]
            send_ref[2 * s + j] = chip + (1.0 - mine) * keep_ref[2 * s + j]
        if with_gain:
            for half in range(2):
                at = 8 * half + 2 * s
                refs[-1][at : at + 2] = slots[s][MAIN + 2 * half : MAIN + 2 * half + 2]


def struct(dtype, *shape):
    return jax.ShapeDtypeStruct(shape, dtype)


MATMUL = 2 * 128**3


def call(kernel, outs, matmuls, *args, scratch=(), spec=None, limit=8 << 20):
    vmem = pl.BlockSpec(memory_space=pltpu.VMEM)
    moved = sum(a.size * a.dtype.itemsize for a in args)
    return pl.pallas_call(
        kernel,
        out_shape=outs,
        in_specs=[spec or vmem] * len(args),
        out_specs=[vmem] * len(outs),
        scratch_shapes=list(scratch),
        compiler_params=pltpu.CompilerParams(vmem_limit_bytes=limit),
        cost_estimate=pl.CostEstimate(
            flops=matmuls * MATMUL, bytes_accessed=moved, transcendentals=0
        ),
    )(*args)


def tie(*values):
    return lax.optimization_barrier(values)


def shift_x(value, s):
    return lax.ppermute(value, "x", [(i, (i + s) % NX) for i in range(NX)])


def flip(value, axis, bits):
    return lax.ppermute(value, axis, [(i, i ^ bits) for i in range(lax.axis_size(axis))])


def shift_z(value, places, reverse):
    pairs = []
    for z in range(NZ):
        for c in range(NC):
            way = (1 if c == 0 else -1) * (-1 if reverse else 1)
            pairs.append((z * NC + c, ((z + way * places) % NZ) * NC + c))
    return lax.ppermute(value, ("z", "core"), pairs)


def device_sum(keep, send, reverse, beside, gain=None):
    with_gain = gain is not None
    more = 8 if with_gain else 0
    rows = struct(F32, MAIN + more, HEAD)
    half = struct(F32, 8, HEAD, HEAD)

    got = flip(send, "core", 1)
    extra = ()
    if with_gain:
        extra = (gain, flip(gain, "dp", 1))
    keep = keep(send)
    got, keep, *extra = tie(got, keep, *extra)
    total = call(
        functools.partial(total_kernel, with_gain), [rows] * NX, 0, keep, got, *extra
    )
    third, second, first = (shift_x(total[s], s) for s in (3, 2, 1))
    first, second, third = beside("x", total[0], first, second, third)
    parts = (total[0], first, second, third)
    whole = (parts[0] + parts[1]) + (parts[2] + parts[3])

    behind, ahead = tie(shift_z(whole, 1, reverse), shift_z(whole, -1, reverse))
    triple, pair = call(
        functools.partial(message_kernel, reverse, with_gain),
        [struct(F32, MAIN + 2 * more, HEAD), rows], 0, whole, behind, ahead,
    )
    three, two = tie(shift_z(triple, 3, reverse), shift_z(pair, -2, reverse))
    chip = call(
        functools.partial(chip_kernel, reverse, with_gain),
        [rows] * NX + ([] if with_gain else [struct(F32, 2, HEAD, HEAD)]), 0,
        whole, behind, ahead, three, two, *parts, got,
        scratch=[pltpu.VMEM((NZ, 4, HEAD), F32)] if with_gain else [],
    )
    third, second, first = (shift_x(chip[s], s) for s in (3, 2, 1))
    first, second, third = beside("back", chip[-1], first, second, third)
    own, back, *gain_rows = call(
        functools.partial(last_kernel, reverse, with_gain),
        [half, half] + ([struct(F32, HEADS, HEAD)] if with_gain else []), 0,
        chip[0], third, second, first, keep, got,
    )
    other = flip(back, "core", 1)
    (other, *gain_rows) = beside("core", own, other, *gain_rows)
    return own, other, gain_rows


def per_device(queries, keys, values, out_grad, gain):
    q, k, v, g = (a.reshape(GROUP, WIDTH) for a in (queries, keys, values, out_grad))
    gain = gain.reshape(1, WIDTH)
    kept = {}
    half = struct(F32, 8, HEAD, HEAD)
    full = struct(F32, HEADS, GROUP, HEAD)

    def heads16(n):
        return struct(BF16, n, GROUP, HEAD)

    def norm_own(positions, first, state):
        n = len(positions)
        return call(
            functools.partial(own_norm_kernel, positions, first),
            [heads16(n), heads16(n), struct(F32, n, HEAD)], 2 * n,
            q, g, gain, kept["local"][1], state,
            scratch=[pltpu.VMEM((n, GROUP, HEAD), F32)],
        )

    def beside_first(stage, ready, *results):
        if stage == "x":
            late, _ = tie(q, ready)
            work = call(local_kernel, [heads16(HEADS), full], 2 * HEADS, late, k, v)
            name = "local"
        elif stage == "back":
            work, name = norm_own((0, 1), 0, ready), "a"
        else:
            work, name = norm_own(tuple(range(2, 8)), 0, ready), "b"
        tied = tie(*results, *work)
        kept[name] = tied[len(results) :]
        return tied[: len(results)]

    (send,) = call(
        send_kernel, [half], 8, k, v,
        scratch=[
            pltpu.VMEM((GROUP, WIDTH // 2), BF16),
            pltpu.VMEM((GROUP, WIDTH // 2), BF16),
            pltpu.SemaphoreType.DMA((2,)),
        ],
        spec=pl.BlockSpec(memory_space=pltpu.MemorySpace.HBM),
        limit=56_000_000,
    )

    def keep_first(ready):
        late, _ = tie(k, ready)
        return call(keep_kernel, [half], 8, late, v)[0]

    own, other, _ = device_sum(keep_first, send, False, beside_first)
    weights, local = kept["local"]
    normed_a, grad_a, sums_a = kept["a"]
    normed_b, grad_b, sums_b = kept["b"]
    normed_c, grad_c, send, gain_rows = call(
        other_norm_kernel,
        [heads16(8), heads16(8), half, struct(F32, NX, 8, HEAD)], 24,
        q, g, gain, local, other, sums_a, sums_b,
        scratch=[pltpu.VMEM((8, GROUP, HEAD), F32)],
    )

    def keep_second(ready):
        late, _ = tie(q, ready)
        return call(own_outer_kernel, [half], 8, late, grad_a, grad_b)[0]

    def beside_second(stage, ready, *results):
        if stage == "x":
            late, _ = tie(q, ready)
            work = call(
                query_kernel,
                [struct(BF16, GROUP, WIDTH), struct(BF16, GROUP, WIDTH), full, full], 6 * HEADS,
                late, k, v, weights, own, other,
                grad_a, grad_b, grad_c, normed_a, normed_b, normed_c,
                scratch=[pltpu.VMEM((HEADS, GROUP, GROUP), BF16)],
            )
            name = "query"
        elif stage == "back":
            return tie(*results)
        else:
            _, _, key_part, value_part = kept["query"]
            work = call(
                own_key_kernel, [heads16(8), heads16(8)], 32,
                k, v, key_part, value_part, ready,
            )
            name = "key"
            other_state, rows = results
            results = (other_state, rows + cross_cores(rows))
        tied = tie(*results, *work)
        kept[name] = tied[len(results) :]
        return tied[: len(results)]

    def cross_cores(rows):
        crossed = flip(rows.reshape(2, 8, HEAD), "core", 1)
        return crossed[::-1].reshape(HEADS, HEAD)

    _, later_other, (rows,) = device_sum(
        keep_second, send, True, beside_second, gain_rows
    )
    rows = rows + flip(rows, "dp", 3)
    normed_out, query_grad, key_part, value_part = kept["query"]
    key_grad, value_grad = call(
        other_key_kernel, [struct(BF16, GROUP, WIDTH), struct(BF16, GROUP, WIDTH)], 32,
        k, v, key_part, value_part, later_other, *kept["key"],
    )
    (gain_grad,) = call(scale_kernel, [struct(F32, 1, WIDTH)], 0, rows)
    shape = queries.shape
    return (
        normed_out.reshape(shape),
        query_grad.reshape(shape),
        key_grad.reshape(shape),
        value_grad.reshape(shape),
        gain_grad.reshape(WIDTH),
    )


def solution(mesh):
    fine = Mesh(mesh.devices.reshape(NZ, NX, NC, NY), ("z", "x", "core", "dp"))
    rows = P("dp", ("z", "x", "core"), None)
    return jax.shard_map(
        per_device,
        mesh=fine,
        in_specs=(rows, rows, rows, rows, P()),
        out_specs=(rows, rows, rows, rows, P()),
        check_vma=False,
    )
```

```python
import functools
import math

import jax
import jax.numpy as jnp
from jax import lax
from jax.experimental import pallas as pl
from jax.experimental.pallas import tpu as pltpu
from jax.sharding import Mesh, PartitionSpec as P


HEAD = 128
HEADS = 16
GROUP = 128
WIDTH = HEAD * HEADS
NZ, NX, NC, NY = 8, 4, 2, 4
TOKENS = GROUP * NZ * NX * NC * NY
F32 = jnp.float32
BF16 = jnp.bfloat16


OWN = tuple(range(8))
OTHER = tuple(range(8, 16))
MAIN = 2 * HEAD
GAIN_TERMS = ((0, 0, 0), (1, 0, -1), (2, 0, 1), (3, 0, -3), (3, 4, -4), (3, 8, -2), (4, 0, 2), (4, 4, 3))


def dot(a, b, contract):
    return lax.dot_general(
        a, b, (((contract[0],), (contract[1],)), ((), ())), preferred_element_type=F32
    )


def causal_mask():
    rows = lax.broadcasted_iota(jnp.int32, (GROUP, GROUP), 0)
    cols = lax.broadcasted_iota(jnp.int32, (GROUP, GROUP), 1)
    return rows >= cols


def here():
    return lax.axis_index("z"), lax.axis_index("x"), lax.axis_index("core")


def first_column(p):
    _, x, c = here()
    head = (c ^ (p // 8)) * 8 + ((x + (p % 8) // 2) & 3) * 2 + p % 2
    return head * HEAD


def columns(p):
    return pl.ds(pl.multiple_of(first_column(p), HEAD), HEAD)


def split_state(state, axis):
    high = state.astype(BF16)
    low = (state - high.astype(F32)).astype(BF16)
    return jnp.concatenate([high, low], axis=axis)


def twice(value):
    return jnp.concatenate([value, value], axis=1)


def one_if(flag):
    return jnp.where(flag, 1.0, 0.0).astype(F32)


def send_kernel(k_hbm, v_hbm, out_ref, k_half, v_half, sems):
    first = pl.multiple_of((1 - here()[2]) * (WIDTH // 2), WIDTH // 2)
    half = pl.ds(first, WIDTH // 2)
    copies = (
        pltpu.make_async_copy(k_hbm.at[:, half], k_half, sems.at[0]),
        pltpu.make_async_copy(v_hbm.at[:, half], v_half, sems.at[1]),
    )
    for copy in copies:
        copy.start()
    for copy in copies:
        copy.wait()
    for p in OTHER:
        at = pl.ds(pl.multiple_of(first_column(p) - first, HEAD), HEAD)
        out_ref[p - 8] = dot(k_half[:, at], v_half[:, at], (0, 0))


def keep_kernel(k_ref, v_ref, out_ref):
    for p in OWN:
        at = columns(p)
        out_ref[p] = dot(k_ref[:, at], v_ref[:, at], (0, 0))


def local_kernel(q_ref, k_ref, v_ref, weights_ref, attended_ref):
    causal = causal_mask()
    for p in range(HEADS):
        at = columns(p)
        scores = dot(q_ref[:, at], k_ref[:, at], (1, 1))
        weights_ref[p] = jnp.where(causal, scores, 0.0).astype(BF16)
    for p in range(HEADS):
        attended_ref[p] = dot(weights_ref[p], v_ref[:, columns(p)], (1, 0))


def norm_rows(positions, q_ref, g_ref, gain_ref, local_ref, state_ref, first, normed_ref, grad_ref, attended_ref, store):
    for i, p in enumerate(positions):
        both = split_state(state_ref[p - first], 0)
        attended_ref[i] = local_ref[p] + dot(twice(q_ref[:, columns(p)]), both, (1, 0))
    for i, p in enumerate(positions):
        at = columns(p)
        attended = attended_ref[i]
        inv_rms = lax.rsqrt(jnp.mean(attended * attended, axis=1, keepdims=True) + 1e-05)
        normed = attended * inv_rms
        gain = gain_ref[:, at]
        normed_ref[i] = (normed * gain).astype(BF16)
        grad_wide = g_ref[:, at].astype(F32)
        product = normed * grad_wide
        store(i, jnp.sum(product, axis=0, keepdims=True))
        along = jnp.mean(product * gain, axis=1, keepdims=True)
        grad_ref[i] = (inv_rms * (grad_wide * gain - normed * along)).astype(BF16)


def own_norm_kernel(
    positions, first, q_ref, g_ref, gain_ref, local_ref, state_ref,
    normed_ref, grad_ref, sums_ref, attended_ref,
):
    def store(i, value):
        sums_ref[i : i + 1] = value

    norm_rows(positions, q_ref, g_ref, gain_ref, local_ref, state_ref, first, normed_ref, grad_ref, attended_ref, store)


def other_norm_kernel(
    q_ref, g_ref, gain_ref, local_ref, state_ref, sums_a_ref, sums_b_ref,
    normed_ref, grad_ref, gain_rows_ref, attended_ref,
):
    def store(i, value):
        gain_rows_ref[i // 2, 2 + i % 2 : 3 + i % 2] = value

    norm_rows(OTHER, q_ref, g_ref, gain_ref, local_ref, state_ref, 8, normed_ref, grad_ref, attended_ref, store)
    for s in range(NX):
        gain_rows_ref[s, 0:2] = sums_a_ref[...] if s == 0 else sums_b_ref[2 * s - 2 : 2 * s]
        gain_rows_ref[s, 4:8] = jnp.zeros((4, HEAD), F32)


def other_outer_kernel(q_ref, grad_ref, send_ref):
    for i, p in enumerate(OTHER):
        send_ref[i] = dot(q_ref[:, columns(p)], grad_ref[i], (0, 0))


def own_outer_kernel(q_ref, grad_a_ref, grad_b_ref, keep_ref):
    for p in OWN:
        grad = grad_a_ref[p] if p < 2 else grad_b_ref[p - 2]
        keep_ref[p] = dot(q_ref[:, columns(p)], grad, (0, 0))


def query_kernel(
    q_ref, k_ref, v_ref, weights_ref, own_ref, other_ref,
    grad_a_ref, grad_b_ref, grad_c_ref, normed_a_ref, normed_b_ref, normed_c_ref,
    normed_out_ref, query_grad_ref, key_part_ref, value_part_ref, mixed_ref,
):
    causal = causal_mask()

    def of(p, a_ref, b_ref, c_ref):
        return a_ref[p] if p < 2 else b_ref[p - 2] if p < 8 else c_ref[p - 8]

    def grad(p):
        return of(p, grad_a_ref, grad_b_ref, grad_c_ref)

    for p in range(HEADS):
        at = columns(p)
        normed_out_ref[:, at] = of(p, normed_a_ref, normed_b_ref, normed_c_ref)
        mixed_ref[p] = jnp.where(causal, dot(grad(p), v_ref[:, at], (1, 1)), 0.0).astype(BF16)
    for p in range(HEADS):
        at = columns(p)
        both = split_state((own_ref if p < 8 else other_ref)[p % 8], 1)
        query_grad_ref[:, at] = (
            dot(mixed_ref[p], k_ref[:, at], (1, 0)) + dot(twice(grad(p)), both, (1, 1))
        ).astype(BF16)
        key_part_ref[p] = dot(mixed_ref[p], q_ref[:, at], (0, 0))
        value_part_ref[p] = dot(weights_ref[p], grad(p), (0, 0))


def key_rows(p, k_ref, v_ref, key_part_ref, value_part_ref, state):
    at = columns(p)
    key = key_part_ref[p] + dot(twice(v_ref[:, at]), split_state(state, 1), (1, 1))
    value = value_part_ref[p] + dot(twice(k_ref[:, at]), split_state(state, 0), (1, 0))
    return key.astype(BF16), value.astype(BF16)


def own_key_kernel(k_ref, v_ref, key_part_ref, value_part_ref, state_ref, key_ref, value_ref):
    for p in OWN:
        key_ref[p], value_ref[p] = key_rows(
            p, k_ref, v_ref, key_part_ref, value_part_ref, state_ref[p]
        )


def other_key_kernel(
    k_ref, v_ref, key_part_ref, value_part_ref, state_ref, own_key_ref, own_value_ref,
    key_grad_ref, value_grad_ref,
):
    for p in OWN:
        at = columns(p)
        key_grad_ref[:, at] = own_key_ref[p]
        value_grad_ref[:, at] = own_value_ref[p]
    for p in OTHER:
        at = columns(p)
        key_grad_ref[:, at], value_grad_ref[:, at] = key_rows(
            p, k_ref, v_ref, key_part_ref, value_part_ref, state_ref[p - 8]
        )


def scale_kernel(rows_ref, out_ref):
    for p in range(HEADS):
        out_ref[:, columns(p)] = rows_ref[p : p + 1] / math.sqrt(TOKENS)


def along_scan(reverse):
    y = NZ - 1 - here()[0] if reverse else here()[0]
    return y, 1 - 2 * here()[2]


def total_kernel(with_gain, *refs):
    keep_ref, got_ref = refs[:2]
    outs = refs[-NX:]
    for s in range(NX):
        for j in range(2):
            outs[s][j * HEAD : (j + 1) * HEAD] = keep_ref[2 * s + j] + got_ref[2 * s + j]
        if with_gain:
            outs[s][MAIN : MAIN + 8] = refs[2][s] + refs[3][s]


def message_kernel(reverse, with_gain, whole_ref, behind_ref, ahead_ref, three_ref, two_ref):
    y, way = along_scan(reverse)
    further, back = (y + 3 * way) & 7, (y - 2 * way) & 7
    whole, behind, ahead = whole_ref[:MAIN], behind_ref[:MAIN], ahead_ref[:MAIN]
    before, after = (y - way) & 7, (y + way) & 7
    three_ref[:MAIN] = (
        one_if(y < further) * whole + one_if(before < further) * behind + one_if(after < further) * ahead
    )
    two_ref[:MAIN] = one_if(y < back) * whole + one_if(after < back) * ahead
    if with_gain:
        for i, ref in enumerate((whole_ref, behind_ref, ahead_ref)):
            three_ref[MAIN + 4 * i : MAIN + 4 * i + 4] = ref[MAIN : MAIN + 4]
        three_ref[MAIN + 12 : MAIN + 16] = jnp.zeros((4, HEAD), F32)
        for i, ref in enumerate((whole_ref, ahead_ref)):
            two_ref[MAIN + 4 * i : MAIN + 4 * i + 4] = ref[MAIN : MAIN + 4]


def chip_kernel(reverse, with_gain, *refs):
    _, behind_ref, ahead_ref, three_ref, two_ref = refs[:5]
    parts, got_ref = refs[5:9], refs[9]
    outs, own_ref = refs[10:14], refs[14]
    y, way = along_scan(reverse)
    base = (
        one_if(((y - way) & 7) < y) * behind_ref[:MAIN]
        + one_if(((y + way) & 7) < y) * ahead_ref[:MAIN]
        + (three_ref[:MAIN] + two_ref[:MAIN])
    )
    x = here()[1]
    for s in range(NX):
        value = base
        target = (x + s) & 3
        for t in range(NX):
            source = (x - t) & 3
            flag = source > target if reverse else source < target
            value = value + one_if(flag) * parts[t][:MAIN]
        outs[s][:MAIN] = value
        if s == 0 and not with_gain:
            mine = one_if(here()[2] == (0 if reverse else 1))
            for j in range(2):
                own_ref[j] = value[j * HEAD : (j + 1) * HEAD] + mine * got_ref[j]
    if with_gain:
        by_place = refs[14]
        for which, row, further in GAIN_TERMS:
            by_place[(y + further * way) & 7] = refs[which][MAIN + row : MAIN + row + 4]
        total = by_place[0]
        for i in range(1, NZ):
            total = total + by_place[i]
        for s in range(NX):
            outs[s][MAIN : MAIN + 4] = total
            outs[s][MAIN + 4 : MAIN + 8] = jnp.zeros_like(total)


def last_kernel(reverse, with_gain, *refs):
    slots, keep_ref, got_ref = refs[:NX], refs[NX], refs[NX + 1]
    own_ref, send_ref = refs[NX + 2], refs[NX + 3]
    mine = one_if(here()[2] == (0 if reverse else 1))
    for s in range(NX):
        for j in range(2):
            chip = slots[s][j * HEAD : (j + 1) * HEAD]
            own_ref[2 * s + j] = chip + mine * got_ref[2 * s + j]
            send_ref[2 * s + j] = chip + (1.0 - mine) * keep_ref[2 * s + j]
        if with_gain:
            for half in range(2):
                at = 8 * half + 2 * s
                refs[-1][at : at + 2] = slots[s][MAIN + 2 * half : MAIN + 2 * half + 2]


def struct(dtype, *shape):
    return jax.ShapeDtypeStruct(shape, dtype)


MATMUL = 2 * 128**3


def call(kernel, outs, matmuls, *args, scratch=(), spec=None, limit=8 << 20):
    vmem = pl.BlockSpec(memory_space=pltpu.VMEM)
    moved = sum(a.size * a.dtype.itemsize for a in args)
    return pl.pallas_call(
        kernel,
        out_shape=outs,
        in_specs=[spec or vmem] * len(args),
        out_specs=[vmem] * len(outs),
        scratch_shapes=list(scratch),
        compiler_params=pltpu.CompilerParams(vmem_limit_bytes=limit),
        cost_estimate=pl.CostEstimate(
            flops=matmuls * MATMUL, bytes_accessed=moved, transcendentals=0
        ),
    )(*args)


def tie(*values):
    return lax.optimization_barrier(values)


def shift_x(value, s):
    return lax.ppermute(value, "x", [(i, (i + s) % NX) for i in range(NX)])


def flip(value, axis, bits):
    return lax.ppermute(value, axis, [(i, i ^ bits) for i in range(lax.axis_size(axis))])


def shift_z(value, places, reverse):
    pairs = []
    for z in range(NZ):
        for c in range(NC):
            way = (1 if c == 0 else -1) * (-1 if reverse else 1)
            pairs.append((z * NC + c, ((z + way * places) % NZ) * NC + c))
    return lax.ppermute(value, ("z", "core"), pairs)


def device_sum(keep, send, reverse, beside, gain=None):
    with_gain = gain is not None
    more = 8 if with_gain else 0
    rows = struct(F32, MAIN + more, HEAD)
    half = struct(F32, 8, HEAD, HEAD)

    got = flip(send, "core", 1)
    extra = ()
    if with_gain:
        extra = (gain, flip(gain, "dp", 1))
    keep = keep(send)
    got, keep, *extra = tie(got, keep, *extra)
    total = call(
        functools.partial(total_kernel, with_gain), [rows] * NX, 0, keep, got, *extra
    )
    third, second, first = (shift_x(total[s], s) for s in (3, 2, 1))
    first, second, third = beside("x", total[0], first, second, third)
    parts = (total[0], first, second, third)
    whole = (parts[0] + parts[1]) + (parts[2] + parts[3])

    behind, ahead = tie(shift_z(whole, 1, reverse), shift_z(whole, -1, reverse))
    triple, pair = call(
        functools.partial(message_kernel, reverse, with_gain),
        [struct(F32, MAIN + 2 * more, HEAD), rows], 0, whole, behind, ahead,
    )
    three, two = tie(shift_z(triple, 3, reverse), shift_z(pair, -2, reverse))
    chip = call(
        functools.partial(chip_kernel, reverse, with_gain),
        [rows] * NX + ([] if with_gain else [struct(F32, 2, HEAD, HEAD)]), 0,
        whole, behind, ahead, three, two, *parts, got,
        scratch=[pltpu.VMEM((NZ, 4, HEAD), F32)] if with_gain else [],
    )
    third, second, first = (shift_x(chip[s], s) for s in (3, 2, 1))
    first, second, third = beside("back", chip[-1], first, second, third)
    own, back, *gain_rows = call(
        functools.partial(last_kernel, reverse, with_gain),
        [half, half] + ([struct(F32, HEADS, HEAD)] if with_gain else []), 0,
        chip[0], third, second, first, keep, got,
    )
    other = flip(back, "core", 1)
    (other, *gain_rows) = beside("core", own, other, *gain_rows)
    return own, other, gain_rows


def compute(queries, keys, values, out_grad, gain):
    q, k, v, g = (a.reshape(GROUP, WIDTH) for a in (queries, keys, values, out_grad))
    gain = gain.reshape(1, WIDTH)
    kept = {}
    half = struct(F32, 8, HEAD, HEAD)
    full = struct(F32, HEADS, GROUP, HEAD)

    def heads16(n):
        return struct(BF16, n, GROUP, HEAD)

    def norm_own(positions, first, state):
        n = len(positions)
        return call(
            functools.partial(own_norm_kernel, positions, first),
            [heads16(n), heads16(n), struct(F32, n, HEAD)], 2 * n,
            q, g, gain, kept["local"][1], state,
            scratch=[pltpu.VMEM((n, GROUP, HEAD), F32)],
        )

    def beside_first(stage, ready, *results):
        if stage == "x":
            late, _ = tie(q, ready)
            work = call(local_kernel, [heads16(HEADS), full], 2 * HEADS, late, k, v)
            name = "local"
        elif stage == "back":
            work, name = norm_own((0, 1), 0, ready), "a"
        else:
            work, name = norm_own(tuple(range(2, 8)), 0, ready), "b"
        tied = tie(*results, *work)
        kept[name] = tied[len(results) :]
        return tied[: len(results)]

    (send,) = call(
        send_kernel, [half], 8, k, v,
        scratch=[
            pltpu.VMEM((GROUP, WIDTH // 2), BF16),
            pltpu.VMEM((GROUP, WIDTH // 2), BF16),
            pltpu.SemaphoreType.DMA((2,)),
        ],
        spec=pl.BlockSpec(memory_space=pltpu.MemorySpace.HBM),
        limit=56_000_000,
    )

    def keep_first(ready):
        late, _ = tie(k, ready)
        return call(keep_kernel, [half], 8, late, v)[0]

    own, other, _ = device_sum(keep_first, send, False, beside_first)
    weights, local = kept["local"]
    normed_a, grad_a, sums_a = kept["a"]
    normed_b, grad_b, sums_b = kept["b"]
    normed_c, grad_c, gain_rows = call(
        other_norm_kernel,
        [heads16(8), heads16(8), struct(F32, NX, 8, HEAD)], 16,
        q, g, gain, local, other, sums_a, sums_b,
        scratch=[pltpu.VMEM((8, GROUP, HEAD), F32)],
    )

    (send,) = call(other_outer_kernel, [half], 8, q, grad_c)

    def keep_second(ready):
        late, _ = tie(q, ready)
        return call(own_outer_kernel, [half], 8, late, grad_a, grad_b)[0]

    def beside_second(stage, ready, *results):
        if stage == "x":
            late, _ = tie(q, ready)
            work = call(
                query_kernel,
                [struct(BF16, GROUP, WIDTH), struct(BF16, GROUP, WIDTH), full, full], 6 * HEADS,
                late, k, v, weights, own, other,
                grad_a, grad_b, grad_c, normed_a, normed_b, normed_c,
                scratch=[pltpu.VMEM((HEADS, GROUP, GROUP), BF16)],
            )
            name = "query"
        elif stage == "back":
            return tie(*results)
        else:
            _, _, key_part, value_part = kept["query"]
            work = call(
                own_key_kernel, [heads16(8), heads16(8)], 32,
                k, v, key_part, value_part, ready,
            )
            name = "key"
            other_state, rows = results
            results = (other_state, rows + cross_cores(rows))
        tied = tie(*results, *work)
        kept[name] = tied[len(results) :]
        return tied[: len(results)]

    def cross_cores(rows):
        crossed = flip(rows.reshape(2, 8, HEAD), "core", 1)
        return crossed[::-1].reshape(HEADS, HEAD)

    _, later_other, (rows,) = device_sum(
        keep_second, send, True, beside_second, gain_rows
    )
    rows = rows + flip(rows, "dp", 3)
    normed_out, query_grad, key_part, value_part = kept["query"]
    key_grad, value_grad = call(
        other_key_kernel, [struct(BF16, GROUP, WIDTH), struct(BF16, GROUP, WIDTH)], 32,
        k, v, key_part, value_part, later_other, *kept["key"],
    )
    (gain_grad,) = call(scale_kernel, [struct(F32, 1, WIDTH)], 0, rows)
    shape = queries.shape
    return (
        normed_out.reshape(shape),
        query_grad.reshape(shape),
        key_grad.reshape(shape),
        value_grad.reshape(shape),
        gain_grad.reshape(WIDTH),
    )


def solution(mesh):
    fine = Mesh(mesh.devices.reshape(NZ, NX, NC, NY), ("z", "x", "core", "dp"))
    rows = P("dp", ("z", "x", "core"), None)
    return jax.shard_map(
        compute,
        mesh=fine,
        in_specs=(rows, rows, rows, rows, P()),
        out_specs=(rows, rows, rows, rows, P()),
        check_vma=False,
    )
```

```python
import functools
import math

import jax
import jax.numpy as jnp
from jax import lax
from jax.experimental import pallas as pl
from jax.experimental.pallas import tpu as pltpu
from jax.sharding import Mesh, PartitionSpec as P

HEAD = 128
HEADS = 16
GROUP = 128
WIDTH = HEAD * HEADS
NZ, NX, NC, NY = 8, 4, 2, 4
TOKENS = GROUP * NZ * NX * NC * NY
F32 = jnp.float32
BF16 = jnp.bfloat16


OWN = tuple(range(8))
OTHER = tuple(range(8, 16))
MAIN = 2 * HEAD
GAIN_TERMS = ((0, 0, 0), (1, 0, -1), (2, 0, 1), (3, 0, -3), (3, 4, -4), (3, 8, -2), (4, 0, 2), (4, 4, 3))


def dot(a, b, contract):
    return lax.dot_general(
        a, b, (((contract[0],), (contract[1],)), ((), ())), preferred_element_type=F32
    )


def causal_mask():
    rows = lax.broadcasted_iota(jnp.int32, (GROUP, GROUP), 0)
    cols = lax.broadcasted_iota(jnp.int32, (GROUP, GROUP), 1)
    return rows >= cols


def here():
    return lax.axis_index("z"), lax.axis_index("x"), lax.axis_index("core")


def first_column(p):
    _, x, c = here()
    head = (c ^ (p // 8)) * 8 + ((x + (p % 8) // 2) & 3) * 2 + p % 2
    return head * HEAD


def columns(p):
    return pl.ds(pl.multiple_of(first_column(p), HEAD), HEAD)


def split_state(state, axis):
    high = state.astype(BF16)
    low = (state - high.astype(F32)).astype(BF16)
    return jnp.concatenate([high, low], axis=axis)


def twice(value):
    return jnp.concatenate([value, value], axis=1)


def one_if(flag):
    return jnp.where(flag, 1.0, 0.0).astype(F32)


def send_kernel(k_hbm, v_hbm, out_ref, k_half, v_half, sems):
    first = pl.multiple_of((1 - here()[2]) * (WIDTH // 2), WIDTH // 2)
    half = pl.ds(first, WIDTH // 2)
    copies = (
        pltpu.make_async_copy(k_hbm.at[:, half], k_half, sems.at[0]),
        pltpu.make_async_copy(v_hbm.at[:, half], v_half, sems.at[1]),
    )
    for copy in copies:
        copy.start()
    for copy in copies:
        copy.wait()
    for p in OTHER:
        at = pl.ds(pl.multiple_of(first_column(p) - first, HEAD), HEAD)
        out_ref[p - 8] = dot(k_half[:, at], v_half[:, at], (0, 0))


def keep_kernel(k_ref, v_ref, out_ref):
    for p in OWN:
        at = columns(p)
        out_ref[p] = dot(k_ref[:, at], v_ref[:, at], (0, 0))


def local_kernel(q_ref, k_ref, v_ref, weights_ref, attended_ref):
    causal = causal_mask()
    for p in range(HEADS):
        at = columns(p)
        scores = dot(q_ref[:, at], k_ref[:, at], (1, 1))
        weights_ref[p] = jnp.where(causal, scores, 0.0).astype(BF16)
    for p in range(HEADS):
        attended_ref[p] = dot(weights_ref[p], v_ref[:, columns(p)], (1, 0))


def norm_rows(positions, q_ref, g_ref, gain_ref, local_ref, state_ref, first, normed_ref, grad_ref, attended_ref, store):
    for i, p in enumerate(positions):
        both = split_state(state_ref[p - first], 0)
        attended_ref[i] = local_ref[p] + dot(twice(q_ref[:, columns(p)]), both, (1, 0))
    for i, p in enumerate(positions):
        at = columns(p)
        attended = attended_ref[i]
        inv_rms = lax.rsqrt(jnp.mean(attended * attended, axis=1, keepdims=True) + 1e-05)
        normed = attended * inv_rms
        gain = gain_ref[:, at]
        normed_ref[i] = (normed * gain).astype(BF16)
        grad_wide = g_ref[:, at].astype(F32)
        product = normed * grad_wide
        store(i, jnp.sum(product, axis=0, keepdims=True))
        along = jnp.mean(product * gain, axis=1, keepdims=True)
        grad_ref[i] = (inv_rms * (grad_wide * gain - normed * along)).astype(BF16)


def own_norm_kernel(
    positions, first, q_ref, g_ref, gain_ref, local_ref, state_ref,
    normed_ref, grad_ref, sums_ref, attended_ref,
):
    def store(i, value):
        sums_ref[i : i + 1] = value

    norm_rows(positions, q_ref, g_ref, gain_ref, local_ref, state_ref, first, normed_ref, grad_ref, attended_ref, store)


def other_norm_kernel(
    q_ref, g_ref, gain_ref, local_ref, state_ref, sums_a_ref, sums_b_ref,
    normed_ref, grad_ref, send_ref, gain_rows_ref, attended_ref,
):
    def store(i, value):
        gain_rows_ref[i // 2, 2 + i % 2 : 3 + i % 2] = value

    norm_rows(OTHER, q_ref, g_ref, gain_ref, local_ref, state_ref, 8, normed_ref, grad_ref, attended_ref, store)
    for i, p in enumerate(OTHER):
        send_ref[i] = dot(q_ref[:, columns(p)], grad_ref[i], (0, 0))
    for s in range(NX):
        gain_rows_ref[s, 0:2] = sums_a_ref[...] if s == 0 else sums_b_ref[2 * s - 2 : 2 * s]
        gain_rows_ref[s, 4:8] = jnp.zeros((4, HEAD), F32)


def own_outer_kernel(q_ref, grad_a_ref, grad_b_ref, keep_ref):
    for p in OWN:
        grad = grad_a_ref[p] if p < 2 else grad_b_ref[p - 2]
        keep_ref[p] = dot(q_ref[:, columns(p)], grad, (0, 0))


def query_kernel(
    q_ref, k_ref, v_ref, weights_ref, own_ref, other_ref,
    grad_a_ref, grad_b_ref, grad_c_ref, normed_a_ref, normed_b_ref, normed_c_ref,
    normed_out_ref, query_grad_ref, key_part_ref, value_part_ref, mixed_ref,
):
    causal = causal_mask()

    def of(p, a_ref, b_ref, c_ref):
        return a_ref[p] if p < 2 else b_ref[p - 2] if p < 8 else c_ref[p - 8]

    def grad(p):
        return of(p, grad_a_ref, grad_b_ref, grad_c_ref)

    for p in range(HEADS):
        at = columns(p)
        normed_out_ref[:, at] = of(p, normed_a_ref, normed_b_ref, normed_c_ref)
        mixed_ref[p] = jnp.where(causal, dot(grad(p), v_ref[:, at], (1, 1)), 0.0).astype(BF16)
    for p in range(HEADS):
        at = columns(p)
        both = split_state((own_ref if p < 8 else other_ref)[p % 8], 1)
        query_grad_ref[:, at] = (
            dot(mixed_ref[p], k_ref[:, at], (1, 0)) + dot(twice(grad(p)), both, (1, 1))
        ).astype(BF16)
        key_part_ref[p] = dot(mixed_ref[p], q_ref[:, at], (0, 0))
        value_part_ref[p] = dot(weights_ref[p], grad(p), (0, 0))


def key_rows(p, k_ref, v_ref, key_part_ref, value_part_ref, state):
    at = columns(p)
    key = key_part_ref[p] + dot(twice(v_ref[:, at]), split_state(state, 1), (1, 1))
    value = value_part_ref[p] + dot(twice(k_ref[:, at]), split_state(state, 0), (1, 0))
    return key.astype(BF16), value.astype(BF16)


def own_key_kernel(k_ref, v_ref, key_part_ref, value_part_ref, state_ref, key_ref, value_ref):
    for p in OWN:
        key_ref[p], value_ref[p] = key_rows(
            p, k_ref, v_ref, key_part_ref, value_part_ref, state_ref[p]
        )


def other_key_kernel(
    k_ref, v_ref, key_part_ref, value_part_ref, state_ref, own_key_ref, own_value_ref,
    key_grad_ref, value_grad_ref,
):
    for p in OWN:
        at = columns(p)
        key_grad_ref[:, at] = own_key_ref[p]
        value_grad_ref[:, at] = own_value_ref[p]
    for p in OTHER:
        at = columns(p)
        key_grad_ref[:, at], value_grad_ref[:, at] = key_rows(
            p, k_ref, v_ref, key_part_ref, value_part_ref, state_ref[p - 8]
        )


def scale_kernel(rows_ref, out_ref):
    for p in range(HEADS):
        out_ref[:, columns(p)] = rows_ref[p : p + 1] / math.sqrt(TOKENS)


def along_scan(reverse):
    y = NZ - 1 - here()[0] if reverse else here()[0]
    return y, 1 - 2 * here()[2]


def total_kernel(with_gain, *refs):
    keep_ref, got_ref = refs[:2]
    outs = refs[-NX:]
    for s in range(NX):
        for j in range(2):
            outs[s][j * HEAD : (j + 1) * HEAD] = keep_ref[2 * s + j] + got_ref[2 * s + j]
        if with_gain:
            outs[s][MAIN : MAIN + 8] = refs[2][s] + refs[3][s]


def message_kernel(reverse, with_gain, whole_ref, behind_ref, ahead_ref, three_ref, two_ref):
    y, way = along_scan(reverse)
    further, back = (y + 3 * way) & 7, (y - 2 * way) & 7
    whole, behind, ahead = whole_ref[:MAIN], behind_ref[:MAIN], ahead_ref[:MAIN]
    before, after = (y - way) & 7, (y + way) & 7
    three_ref[:MAIN] = (
        one_if(y < further) * whole + one_if(before < further) * behind + one_if(after < further) * ahead
    )
    two_ref[:MAIN] = one_if(y < back) * whole + one_if(after < back) * ahead
    if with_gain:
        for i, ref in enumerate((whole_ref, behind_ref, ahead_ref)):
            three_ref[MAIN + 4 * i : MAIN + 4 * i + 4] = ref[MAIN : MAIN + 4]
        three_ref[MAIN + 12 : MAIN + 16] = jnp.zeros((4, HEAD), F32)
        for i, ref in enumerate((whole_ref, ahead_ref)):
            two_ref[MAIN + 4 * i : MAIN + 4 * i + 4] = ref[MAIN : MAIN + 4]


def chip_kernel(reverse, with_gain, *refs):
    whole_ref, behind_ref, ahead_ref, three_ref, two_ref = refs[:5]
    parts, got_ref = refs[5:9], refs[9]
    outs, own_ref = refs[10:14], refs[14]
    y, way = along_scan(reverse)
    base = (
        one_if(((y - way) & 7) < y) * behind_ref[:MAIN]
        + one_if(((y + way) & 7) < y) * ahead_ref[:MAIN]
        + (three_ref[:MAIN] + two_ref[:MAIN])
    )
    x = here()[1]
    for s in range(NX):
        value = base
        target = (x + s) & 3
        for t in range(NX):
            source = (x - t) & 3
            flag = source > target if reverse else source < target
            value = value + one_if(flag) * parts[t][:MAIN]
        outs[s][:MAIN] = value
        if s == 0 and not with_gain:
            mine = one_if(here()[2] == (0 if reverse else 1))
            for j in range(2):
                own_ref[j] = value[j * HEAD : (j + 1) * HEAD] + mine * got_ref[j]
    if with_gain:
        by_place = refs[14]
        for which, row, further in GAIN_TERMS:
            by_place[(y + further * way) & 7] = refs[which][MAIN + row : MAIN + row + 4]
        total = by_place[0]
        for i in range(1, NZ):
            total = total + by_place[i]
        for s in range(NX):
            outs[s][MAIN : MAIN + 4] = total
            outs[s][MAIN + 4 : MAIN + 8] = jnp.zeros_like(total)


def last_kernel(reverse, with_gain, *refs):
    slots, keep_ref, got_ref = refs[:NX], refs[NX], refs[NX + 1]
    own_ref, send_ref = refs[NX + 2], refs[NX + 3]
    mine = one_if(here()[2] == (0 if reverse else 1))
    for s in range(NX):
        for j in range(2):
            chip = slots[s][j * HEAD : (j + 1) * HEAD]
            own_ref[2 * s + j] = chip + mine * got_ref[2 * s + j]
            send_ref[2 * s + j] = chip + (1.0 - mine) * keep_ref[2 * s + j]
        if with_gain:
            for half in range(2):
                at = 8 * half + 2 * s
                refs[-1][at : at + 2] = slots[s][MAIN + 2 * half : MAIN + 2 * half + 2]


def struct(dtype, *shape):
    return jax.ShapeDtypeStruct(shape, dtype)


MATMUL = 2 * 128**3


def call(kernel, outs, matmuls, *args, scratch=(), spec=None, limit=8 << 20):
    vmem = pl.BlockSpec(memory_space=pltpu.VMEM)
    moved = sum(a.size * a.dtype.itemsize for a in args)
    return pl.pallas_call(
        kernel,
        out_shape=outs,
        in_specs=[spec or vmem] * len(args),
        out_specs=[vmem] * len(outs),
        scratch_shapes=list(scratch),
        compiler_params=pltpu.CompilerParams(vmem_limit_bytes=limit),
        cost_estimate=pl.CostEstimate(
            flops=matmuls * MATMUL, bytes_accessed=moved, transcendentals=0
        ),
    )(*args)


def tie(*values):
    return lax.optimization_barrier(values)


def shift_x(value, s):
    return lax.ppermute(value, "x", [(i, (i + s) % NX) for i in range(NX)])


def flip(value, axis, bits):
    return lax.ppermute(value, axis, [(i, i ^ bits) for i in range(lax.axis_size(axis))])


def shift_z(value, places, reverse):
    pairs = []
    for z in range(NZ):
        for c in range(NC):
            way = (1 if c == 0 else -1) * (-1 if reverse else 1)
            pairs.append((z * NC + c, ((z + way * places) % NZ) * NC + c))
    return lax.ppermute(value, ("z", "core"), pairs)


def device_sum(keep, send, reverse, beside, gain=None):
    with_gain = gain is not None
    more = 8 if with_gain else 0
    rows = struct(F32, MAIN + more, HEAD)
    half = struct(F32, 8, HEAD, HEAD)

    got = flip(send, "core", 1)
    extra = ()
    if with_gain:
        extra = (gain, flip(gain, "dp", 1))
    keep = keep(send)
    got, keep, *extra = tie(got, keep, *extra)
    total = call(
        functools.partial(total_kernel, with_gain), [rows] * NX, 0, keep, got, *extra
    )
    third, second, first = (shift_x(total[s], s) for s in (3, 2, 1))
    first, second, third = beside("x", total[0], first, second, third)
    parts = (total[0], first, second, third)
    whole = (parts[0] + parts[1]) + (parts[2] + parts[3])

    behind, ahead = tie(shift_z(whole, 1, reverse), shift_z(whole, -1, reverse))
    triple, pair = call(
        functools.partial(message_kernel, reverse, with_gain),
        [struct(F32, MAIN + 2 * more, HEAD), rows], 0, whole, behind, ahead,
    )
    three, two = tie(shift_z(triple, 3, reverse), shift_z(pair, -2, reverse))
    chip = call(
        functools.partial(chip_kernel, reverse, with_gain),
        [rows] * NX + ([] if with_gain else [struct(F32, 2, HEAD, HEAD)]), 0,
        whole, behind, ahead, three, two, *parts, got,
        scratch=[pltpu.VMEM((NZ, 4, HEAD), F32)] if with_gain else [],
    )
    third, second, first = (shift_x(chip[s], s) for s in (3, 2, 1))
    first, second, third = beside("back", chip[-1], first, second, third)
    own, back, *gain_rows = call(
        functools.partial(last_kernel, reverse, with_gain),
        [half, half] + ([struct(F32, HEADS, HEAD)] if with_gain else []), 0,
        chip[0], third, second, first, keep, got,
    )
    other = flip(back, "core", 1)
    (other, *gain_rows) = beside("core", own, other, *gain_rows)
    return own, other, gain_rows


def per_device(queries, keys, values, out_grad, gain):
    q, k, v, g = (a.reshape(GROUP, WIDTH) for a in (queries, keys, values, out_grad))
    gain = gain.reshape(1, WIDTH)
    kept = {}
    half = struct(F32, 8, HEAD, HEAD)
    full = struct(F32, HEADS, GROUP, HEAD)

    def heads16(n):
        return struct(BF16, n, GROUP, HEAD)

    def norm_own(positions, first, state):
        n = len(positions)
        return call(
            functools.partial(own_norm_kernel, positions, first),
            [heads16(n), heads16(n), struct(F32, n, HEAD)], 2 * n,
            q, g, gain, kept["local"][1], state,
            scratch=[pltpu.VMEM((n, GROUP, HEAD), F32)],
        )

    def beside_first(stage, ready, *results):
        if stage == "x":
            late, _ = tie(q, ready)
            work = call(local_kernel, [heads16(HEADS), full], 2 * HEADS, late, k, v)
            name = "local"
        elif stage == "back":
            work, name = norm_own((0, 1), 0, ready), "a"
        else:
            work, name = norm_own(tuple(range(2, 8)), 0, ready), "b"
        tied = tie(*results, *work)
        kept[name] = tied[len(results) :]
        return tied[: len(results)]

    (send,) = call(
        send_kernel, [half], 8, k, v,
        scratch=[
            pltpu.VMEM((GROUP, WIDTH // 2), BF16),
            pltpu.VMEM((GROUP, WIDTH // 2), BF16),
            pltpu.SemaphoreType.DMA((2,)),
        ],
        spec=pl.BlockSpec(memory_space=pltpu.MemorySpace.HBM),
        limit=56_000_000,
    )

    def keep_first(ready):
        late, _ = tie(k, ready)
        return call(keep_kernel, [half], 8, late, v)[0]

    own, other, _ = device_sum(keep_first, send, False, beside_first)
    weights, local = kept["local"]
    normed_a, grad_a, sums_a = kept["a"]
    normed_b, grad_b, sums_b = kept["b"]
    normed_c, grad_c, send, gain_rows = call(
        other_norm_kernel,
        [heads16(8), heads16(8), half, struct(F32, NX, 8, HEAD)], 24,
        q, g, gain, local, other, sums_a, sums_b,
        scratch=[pltpu.VMEM((8, GROUP, HEAD), F32)],
    )

    def keep_second(ready):
        late, _ = tie(q, ready)
        return call(own_outer_kernel, [half], 8, late, grad_a, grad_b)[0]

    def beside_second(stage, ready, *results):
        if stage == "x":
            late, _ = tie(q, ready)
            work = call(
                query_kernel,
                [struct(BF16, GROUP, WIDTH), struct(BF16, GROUP, WIDTH), full, full], 6 * HEADS,
                late, k, v, weights, own, other,
                grad_a, grad_b, grad_c, normed_a, normed_b, normed_c,
                scratch=[pltpu.VMEM((HEADS, GROUP, GROUP), BF16)],
            )
            name = "query"
        elif stage == "back":
            return tie(*results)
        else:
            _, _, key_part, value_part = kept["query"]
            work = call(
                own_key_kernel, [heads16(8), heads16(8)], 32,
                k, v, key_part, value_part, ready,
            )
            name = "key"
            other_state, rows = results
            kept["rows"] = rows + flip(rows, "dp", 3)
            results = (other_state, rows)
        tied = tie(*results, *work)
        kept[name] = tied[len(results) :]
        return tied[: len(results)]

    def cross_cores(rows):
        crossed = flip(rows.reshape(2, 8, HEAD), "core", 1)
        return crossed[::-1].reshape(HEADS, HEAD)

    _, later_other, (rows,) = device_sum(
        keep_second, send, True, beside_second, gain_rows
    )
    normed_out, query_grad, key_part, value_part = kept["query"]
    key_grad, value_grad = call(
        other_key_kernel, [struct(BF16, GROUP, WIDTH), struct(BF16, GROUP, WIDTH)], 32,
        k, v, key_part, value_part, later_other, *kept["key"],
    )
    rows, key_grad = tie(kept["rows"], key_grad)
    rows = rows + cross_cores(rows)
    (gain_grad,) = call(scale_kernel, [struct(F32, 1, WIDTH)], 0, rows)
    shape = queries.shape
    return (
        normed_out.reshape(shape),
        query_grad.reshape(shape),
        key_grad.reshape(shape),
        value_grad.reshape(shape),
        gain_grad.reshape(WIDTH),
    )


def solution(mesh):
    fine = Mesh(mesh.devices.reshape(NZ, NX, NC, NY), ("z", "x", "core", "dp"))
    rows = P("dp", ("z", "x", "core"), None)
    return jax.shard_map(
        per_device,
        mesh=fine,
        in_specs=(rows, rows, rows, rows, P()),
        out_specs=(rows, rows, rows, rows, P()),
        check_vma=False,
    )
```
